512 devices in a mesh: front: 8 (over x, core), cube: 64 (over y, z).
Axes of the slice: x: 4, y: 4, z: 16, core: 2. Of those that a mesh axis runs over, the one named last changes fastest.
Arguments:
- front: float32 [8, 4096, 4096], P('front', 'cube'), may hold values from -9 to 9, as said below
- own_tiles: float32 [8, 1024, 128, 128], P('front', 'cube'), may hold values from -6 to 6
- partner_tiles: float32 [8, 1024, 128, 128], P('front', 'cube'), may hold values from -6 to 6
- tile_rows: int32 [8, 64, 32, 1], replicated, may hold values from 4 to 31, as said below
- tile_cols: int32 [8, 64, 32], replicated, may hold values from 4 to 31
- live: int32 [8, 64, 2], replicated, may hold values from 8 to 16
Outputs:
- factored: float32 [8, 4096, 4096], P('front', 'cube')
The draws below stay inside these ranges and needn't reach their ends.
Inputs may be any that keep to these rules, and one draw needn't show every extreme that they name: `front`: Symmetric. Its leading 4 * 128 rows and columns form a strictly diagonally dominant block with diagonal entries in 1.2 to 2.5 and off-diagonal entries of magnitude below 1 / 512. `tile_rows`: within the 16 slots of one child on one device for one parent front the tile rows are distinct, dead slots included; over both children's 2 * 16 slots no tile row is named more than 2 times, and in some device's list one is named exactly 2 times.
All inputs are finite; a program needn't handle non-finite values.
Results may differ from the reference program's by a relative error of at most 0.0001.
Values sent between devices are 32-bit elements; how exact they have to be, the bound alone decides.
A program may use at most 64 MiB of HBM per device.

```python
import jax
import jax.numpy as jnp
from jax import lax

F = 4096
TILE = 128
PANELS = 4
TPD = 16
NT = 32
N_FRONT = 8
N_CUBE = 64


def draw_front(key, part):
    key_base, key_near, key_diag = jax.random.split(key, 3)
    shape = (N_FRONT, F, F)
    base_draw = jnp.clip(jax.random.normal(key_base, shape, jnp.float32), -6.0, 6.0)
    symmetric = (base_draw + jnp.swapaxes(base_draw, 1, 2)) * 0.7071
    leading = PANELS * TILE
    near_draw = jax.random.uniform(key_near, shape, jnp.float32, -1.0, 1.0)
    near_draw = (near_draw + jnp.swapaxes(near_draw, 1, 2)) * (0.5 / leading)
    diag_vals = jax.random.uniform(key_diag, (N_FRONT, 1, F), jnp.float32, 1.2, 2.5)
    row_index = jnp.arange(F)[:, None]
    col_index = jnp.arange(F)[None, :]
    in_lead = (row_index < leading) & (col_index < leading)
    crossing = (row_index < leading) != (col_index < leading)
    result = jnp.where(in_lead, near_draw, jnp.where(crossing, symmetric * (1.5 / leading ** 0.5), symmetric))
    on_diag = (row_index == col_index) & (row_index < leading)
    result = jnp.where(on_diag, diag_vals, result)
    return result.astype(jnp.float32)


def draw_tile_rows(key, part):
    count = N_FRONT * N_CUBE * 2
    keys = jax.random.split(jax.random.fold_in(key, 17), count)

    def one_list(single_key):
        return jax.random.permutation(single_key, NT - PANELS)[:TPD]
    lists = jax.vmap(one_list)(keys)
    return (lists.reshape(N_FRONT, N_CUBE, 2 * TPD, 1) + PANELS).astype(jnp.int32)


def place_ends(values, own_key, smallest, high):
    extent = values.shape
    spot = [jax.random.randint(jax.random.fold_in(own_key, axis), (), 0, extent[axis]) for axis in range(len(extent))]
    values = values.at[tuple(spot)].set(smallest)
    longest = extent.index(max(extent))
    spot[longest] = (spot[longest] + 1) % extent[longest]
    return values.at[tuple(spot)].set(high)


def levels(key, extent, cuts, low, high):
    loudness, own = 1.0, jax.random.fold_in(key, 6)
    for position, blocks in cuts:
        heights = jnp.exp(jax.random.uniform(jax.random.fold_in(own, position), (blocks,), jnp.float32, low / len(cuts), high / len(cuts)))
        loudness = loudness * jnp.repeat(heights, extent[position] // blocks).reshape([-1 if axis == position else 1 for axis in range(len(extent))])
    return loudness


def normal_values(key, shape, spread, most, shards=(), held_as=jnp.bfloat16):
    entries = jax.random.normal(key, shape, jnp.float32) * spread
    if len(shards) > 0:
        entries = levels(key, shape, shards, -0.22, 0.18) * entries
    return jnp.clip(entries, min=-most, max=most).astype(held_as)


def setup_inputs(seed: int = 0) -> dict:
    splits = jax.random.split(jax.random.key(seed), 7)
    return {
        "front": draw_front(jax.random.fold_in(splits[6], 71), 0),
        "own_tiles": normal_values(splits[1], (N_FRONT, N_CUBE * TPD, TILE, TILE), 1.0, 6.0, ((0, 8), (1, 64)), jnp.float32),
        "partner_tiles": normal_values(splits[2], (N_FRONT, N_CUBE * TPD, TILE, TILE), 1.0, 6.0, ((0, 8), (1, 64)), jnp.float32),
        "tile_rows": draw_tile_rows(jax.random.fold_in(splits[6], 71), 0),
        "tile_cols": place_ends(jax.random.randint(splits[4], (N_FRONT, N_CUBE, 2 * TPD), PANELS, NT), jax.random.fold_in(splits[4], 1), PANELS, NT - 1).astype(jnp.int32),
        "live": place_ends(jax.random.randint(splits[5], (N_FRONT, N_CUBE, 2), TPD // 2, TPD + 1), jax.random.fold_in(splits[5], 1), TPD // 2, TPD).astype(jnp.int32),
    }


def reference(front, own_tiles, partner_tiles, tile_rows, tile_cols, live):
    results = []
    slot_pos = jnp.arange(TPD)
    row_index = jnp.arange(F)[:, None]
    for front_idx in range(N_FRONT):
        matrix = front[front_idx]
        tiled = matrix.reshape(NT, TILE, NT, TILE).transpose(0, 2, 1, 3)
        for child in range(2):
            if child == 0:
                holdings = own_tiles[front_idx]
            else:
                holdings = partner_tiles[front_idx ^ 1]
            holdings = holdings.reshape(N_CUBE, TPD, TILE, TILE)
            keep_mask = (slot_pos[None, :] < live[front_idx, :, child][:, None]).astype(jnp.float32)
            holdings = holdings * keep_mask[:, :, None, None]
            rows_list = tile_rows[front_idx, :, child * TPD:(child + 1) * TPD, 0].reshape(-1)
            cols_list = tile_cols[front_idx, :, child * TPD:(child + 1) * TPD].reshape(-1)
            tiled = tiled.at[rows_list, cols_list].add(holdings.reshape(-1, TILE, TILE))
        matrix = tiled.transpose(0, 2, 1, 3).reshape(F, F)
        for panel_idx in range(PANELS):
            first = panel_idx * TILE
            panel = matrix[:, first:first + TILE]
            diag_factor = jnp.linalg.cholesky(panel[first:first + TILE])
            all_factor = jax.scipy.linalg.solve_triangular(diag_factor, panel.T, lower=True).T
            masked = jnp.where(row_index >= first + TILE, all_factor, jnp.zeros_like(all_factor))
            matrix = matrix - jnp.dot(masked, masked.T, precision=lax.Precision.HIGHEST)
            placed = all_factor.at[first:first + TILE].set(diag_factor)
            placed = jnp.where(row_index < first, jnp.zeros_like(placed), placed)
            matrix = matrix.at[:, first:first + TILE].set(placed)
        results.append(matrix)
    return jnp.stack(results)
```

```python
import jax
import jax.numpy as jnp
from jax import lax
from jax.experimental import pallas as pl
from jax.experimental.pallas import tpu as pltpu
from jax.sharding import PartitionSpec as P

PANELS = 4
CAP = 2
NY = 4
NZ = 16
HI = lax.Precision.HIGHEST


def swapped(value, axis, apart):
    mask = 2**apart
    pairs = [(source, source ^ mask) for source in range(lax.axis_size(axis))]
    return lax.ppermute(value, axis, pairs)


def route_plan(rows_block, cols_block, tile_size, half_size, rows_dev, tile_count):
    cube_count, count = rows_block.shape
    global_row = rows_block[:, :, None] * tile_size + jnp.arange(2)[None, None, :] * half_size
    global_row = global_row.reshape(cube_count, 2 * count)
    target_dev = global_row // rows_dev
    row_block = global_row % rows_dev // half_size
    piece_cols = jnp.broadcast_to(cols_block[:, :, None], (cube_count, count, 2)).reshape(
        cube_count, 2 * count
    )
    order_pos = jnp.arange(2 * count)
    earlier = order_pos[None, :] < order_pos[:, None]
    same_dest = target_dev[:, :, None] == target_dev[:, None, :]
    slot_rank = jnp.sum(same_dest & earlier[None], axis=2)
    cell_of = row_block * tile_count + piece_cols
    return (target_dev, slot_rank, cell_of)


def pack_sends(holdings, target_dev, slot_rank, position, slot_count, half_size, tile_size):
    cube_count = target_dev.shape[0]
    send_index = lax.dynamic_index_in_dim(target_dev, position, 0, keepdims=False) * slot_count
    send_index = send_index + lax.dynamic_index_in_dim(slot_rank, position, 0, keepdims=False)
    outgoing = jnp.zeros((cube_count * slot_count, half_size, tile_size), jnp.float32)
    outgoing = outgoing.at[send_index].add(holdings.reshape(-1, half_size, tile_size))
    return outgoing.reshape(cube_count, slot_count, half_size, tile_size)


def place_received(
    incoming,
    target_dev,
    slot_rank,
    cell_of,
    position,
    slot_count,
    rows_dev,
    tile_count,
    half_size,
    tile_size,
):
    cube_count = target_dev.shape[0]
    grid_cells = rows_dev // half_size * tile_count
    recv_pos = jnp.arange(cube_count)[:, None] * slot_count + slot_rank
    recv_pos = jnp.where(target_dev == position, recv_pos, cube_count * slot_count)
    placement = jnp.full((cube_count * slot_count,), grid_cells, jnp.int32)
    placement = placement.at[recv_pos.reshape(-1)].set(cell_of.reshape(-1), mode="drop")
    assembled = jnp.zeros((grid_cells, half_size, tile_size), jnp.float32)
    assembled = assembled.at[placement].add(incoming.reshape(-1, half_size, tile_size), mode="drop")
    assembled = assembled.reshape(rows_dev // half_size, tile_count, half_size, tile_size)
    return assembled.transpose(0, 2, 1, 3).reshape(rows_dev, tile_count * tile_size)


def gather_kernel(x_ref, out_ref, own_sem, zr_s, zr_r, zl_s, zl_r, yp_s, yp_r, ym_s, ym_r, fp_s, fp_r, fm_s, fm_r):
    me = lax.axis_index("cube")
    y, z = me // NZ, me % NZ

    def dev(yy, zz):
        return {"cube": yy % NY * NZ + zz % NZ}

    half = x_ref.shape[0] // 2
    barrier = pltpu.get_barrier_semaphore()
    for peer in (dev(y, z + 1), dev(y, z + NZ - 1), dev(y + 1, z), dev(y + NY - 1, z)):
        pl.semaphore_signal(barrier, inc=1, device_id=peer, device_id_type=pl.DeviceIdType.MESH)
    pl.semaphore_wait(barrier, 4)

    def remote(src, dst, send, recv, to):
        return pltpu.make_async_remote_copy(
            src_ref=src, dst_ref=dst, send_sem=send, recv_sem=recv,
            device_id=to, device_id_type=pl.DeviceIdType.MESH,
        )

    def slot(yy, zz):
        return out_ref.at[yy % NY * NZ + zz % NZ]

    def z_of(k):
        return z if k == 0 else (z + NZ - k if k <= 8 else z + k - 8)

    def right(s):
        ref = slot(y, z + NZ - s)
        return remote(ref, ref, zr_s.at[s], zr_r.at[s], dev(y, z + 1))

    def left(s):
        ref = slot(y, z + s)
        return remote(ref, ref, zl_s.at[s], zl_r.at[s], dev(y, z + NZ - 1))

    def y_up(k):
        ref = slot(y, z_of(k))
        return remote(ref, ref, yp_s.at[k], yp_r.at[k], dev(y + 1, z))

    def y_down(k):
        ref = slot(y, z_of(k))
        return remote(ref, ref, ym_s.at[k], ym_r.at[k], dev(y + NY - 1, z))

    def f_up(k):
        ref = slot(y + NY - 1, z_of(k)).at[pl.ds(0, half)]
        return remote(ref, ref, fp_s.at[k], fp_r.at[k], dev(y + 1, z))

    def f_down(k):
        ref = slot(y + 1, z_of(k)).at[pl.ds(half, half)]
        return remote(ref, ref, fm_s.at[k], fm_r.at[k], dev(y + NY - 1, z))

    own = pltpu.make_async_copy(x_ref, out_ref.at[me], own_sem)
    own.start()
    own.wait()
    right(0).start()
    left(0).start()
    y_up(0).start()
    y_down(0).start()

    def forward(k):
        y_up(k).wait_recv()
        f_up(k).start()
        y_down(k).wait_recv()
        f_down(k).start()

    order = [0]
    for s in range(1, 9):
        right(s - 1).wait_recv()
        if s < 8:
            right(s).start()
        y_up(s).start()
        y_down(s).start()
        if s < 8:
            left(s - 1).wait_recv()
            if s < 7:
                left(s).start()
            y_up(s + 8).start()
            y_down(s + 8).start()
        for k in order:
            forward(k)
        order = [s] if s == 8 else [s, s + 8]
    for k in order:
        forward(k)
    for k in range(16):
        f_up(k).wait_recv()
        f_down(k).wait_recv()
        y_up(k).wait_send()
        y_down(k).wait_send()
        f_up(k).wait_send()
        f_down(k).wait_send()
    for s in range(8):
        right(s).wait_send()
    for s in range(7):
        left(s).wait_send()


def gather_panels(own):
    rows, cols = own.shape
    sem = pltpu.SemaphoreType.DMA
    return pl.pallas_call(
        gather_kernel,
        out_shape=jax.ShapeDtypeStruct((NY * NZ, rows, cols), jnp.float32),
        in_specs=[pl.BlockSpec(memory_space=pl.ANY)],
        out_specs=pl.BlockSpec(memory_space=pl.ANY),
        scratch_shapes=[sem, sem((8,)), sem((8,)), sem((7,)), sem((7,))] + [sem((16,))] * 8,
        compiler_params=pltpu.CompilerParams(collective_id=0, has_side_effects=True),
        cost_estimate=pl.CostEstimate(flops=0, bytes_accessed=200_000_000, transcendentals=0),
    )(own)


def factor(lead, tile):
    order = lead.shape[0]
    work = jnp.concatenate([lead, jnp.eye(order, dtype=jnp.float32)], axis=1)
    unit = jnp.eye(tile, dtype=jnp.float32)
    inverse = []
    for k in range(order // tile):
        low = jnp.linalg.cholesky(work[:tile, k * tile:(k + 1) * tile])
        low_inv = jax.scipy.linalg.solve_triangular(low, unit, lower=True)
        done = jnp.dot(low_inv, work[:tile], precision=HI)
        inverse.append(done[:, order:])
        if k + 1 < order // tile:
            below = done[:, (k + 1) * tile:order]
            work = work[tile:] - jnp.dot(below.T, done, precision=HI)
    return jnp.concatenate(inverse, axis=0)


def body(front, own_tiles, partner_tiles, tile_rows, tile_cols, live):
    position = lax.axis_index("cube")
    front_pos = lax.axis_index("front")
    rows_dev = front.shape[1]
    order_size = front.shape[2]
    tile_size = own_tiles.shape[-1]
    half_size = tile_size // 2
    tile_count = order_size // tile_size
    per_device = own_tiles.shape[1]
    lead = PANELS * tile_size
    slot_count = CAP * rows_dev // half_size
    within = jnp.arange(per_device)
    rows_here = lax.dynamic_index_in_dim(tile_rows, front_pos, 0, keepdims=False)[:, :, 0]
    cols_here = lax.dynamic_index_in_dim(tile_cols, front_pos, 0, keepdims=False)
    live_here = lax.dynamic_index_in_dim(live, front_pos, 0, keepdims=False)
    live_mine = lax.dynamic_index_in_dim(live_here, position, 0, keepdims=False)
    arrived = swapped(partner_tiles, "front", 0)
    keep_own = (within < live_mine[0]).astype(jnp.float32)
    keep_arrived = (within < live_mine[1]).astype(jnp.float32)
    holdings = jnp.concatenate(
        [own_tiles[0] * keep_own[:, None, None], arrived[0] * keep_arrived[:, None, None]], axis=0
    )
    target_dev, slot_rank, cell_of = route_plan(
        rows_here, cols_here, tile_size, half_size, rows_dev, tile_count
    )
    outgoing = pack_sends(
        holdings, target_dev, slot_rank, position, slot_count, half_size, tile_size
    )
    incoming = lax.all_to_all(outgoing, "cube", split_axis=0, concat_axis=0, tiled=True)

    own_panel = front[0, :, :lead]
    panels = gather_panels(own_panel).reshape(order_size, lead)
    inverse = factor(panels[:lead], tile_size)
    row_global = position * rows_dev + jnp.arange(rows_dev)[:, None]
    col_global = jnp.arange(lead)[None, :]
    own_factor = jnp.dot(own_panel, inverse.T, precision=HI)
    own_factor = jnp.where(col_global <= row_global, own_factor, 0.0)
    earlier = jnp.where(col_global < row_global // tile_size * tile_size, own_factor, 0.0)
    weights = jnp.dot(earlier, inverse, precision=HI)
    product = jnp.dot(weights, panels[lead:].T, precision=lax.Precision.HIGH)

    added = place_received(
        incoming,
        target_dev,
        slot_rank,
        cell_of,
        position,
        slot_count,
        rows_dev,
        tile_count,
        half_size,
        tile_size,
    )
    rest = front[0, :, lead:] - product + added[:, lead:]
    return jnp.concatenate([own_factor, rest], axis=1)[None]


def solution(mesh):
    in_specs = (
        P("front", "cube", None),
        P("front", "cube", None, None),
        P("front", "cube", None, None),
        P(),
        P(),
        P(),
    )
    out_specs = P("front", "cube", None)
    return jax.shard_map(body, mesh=mesh, in_specs=in_specs, out_specs=out_specs, check_vma=False)
```

```python
import jax
import jax.numpy as jnp
from jax import lax
from jax.experimental import pallas as pl
from jax.experimental.pallas import tpu as pltpu
from jax.sharding import PartitionSpec as P

PANELS = 4
NY = 4
NZ = 16
CELLS = 28
CHUNKS = 4
WIDE = CELLS // CHUNKS
ROUNDS = 6
HIGH = lax.Precision.HIGH
MESH = pl.DeviceIdType.MESH


def exchange_kernel(
    front_ref, own_ref, partner_ref, pick_ref, cols_ref, x_ref, t_ref,
    tiles, packed, ybuf, rbuf, lbuf, first,
    load_sem, pair_s, pair_r, y_s, y_r, r_s, r_r, l_s, l_r,
    zr_s, zr_r, zl_s, zl_r, yp_s, yp_r, ym_s, ym_r, fp_s, fp_r, fm_s, fm_r,
):
    me = lax.axis_index("cube")
    side = lax.axis_index("front")
    y, z = me // NZ, me % NZ
    lead = x_ref.shape[2]
    rows = x_ref.shape[1]
    slots = own_ref.shape[1]
    none = 2 * slots

    def dev(dy, dz):
        return {"cube": (y + dy) % NY * NZ + (z + dz) % NZ}

    mate = {"front": side + 1 - 2 * (side % 2)}
    right, left = dev(0, 1), dev(0, NZ - 1)
    peers = [right, left, dev(1, 0), dev(2, 0), dev(3, 0), mate]
    barrier = pltpu.get_barrier_semaphore()
    for peer in peers:
        pl.semaphore_signal(barrier, inc=1, device_id=peer, device_id_type=MESH)
    pl.semaphore_wait(barrier, len(peers))

    def remote(src, dst, send, recv, to):
        return pltpu.make_async_remote_copy(
            src_ref=src, dst_ref=dst, send_sem=send, recv_sem=recv, device_id=to, device_id_type=MESH
        )

    pair = remote(partner_ref.at[0], tiles.at[pl.ds(slots, slots)], pair_s, pair_r, mate)
    pair.start()
    own = pltpu.make_async_copy(own_ref.at[0], tiles.at[pl.ds(0, slots)], load_sem.at[0])
    own.start()
    mine = pltpu.make_async_copy(front_ref.at[0, :, pl.ds(0, lead)], x_ref.at[me], load_sem.at[1])
    mine.start()
    tiles[none] = jnp.zeros(tiles.shape[1:], jnp.float32)
    own.wait()
    pair.wait()

    def over_y(far, dy):
        return remote(
            packed.at[far, (y + dy) % NY], ybuf.at[far, dy - 1], y_s.at[far, dy - 1], y_r.at[far, dy - 1], dev(dy, 0)
        )

    order = [8]
    for j in range(1, 9):
        order += [8 - j] + ([8 + j] if j < 8 else [])
    for far in order:
        there = (z + far) % NZ
        top = there % 2 * rows
        for to_y in range(NY):
            for child in range(2):
                index = pick_ref[child, to_y * (NZ // 2) + there // 2]
                packed[far, to_y, child] = tiles[index, pl.ds(pl.multiple_of(top, rows), rows), :]
        for dy in range(1, NY):
            over_y(far, dy).start()

    mine.wait()

    def slot(dy, dz):
        return x_ref.at[(y + dy) % NY * NZ + (z + dz) % NZ]

    def z_of(k):
        return 0 if k == 0 else (NZ - k if k <= 8 else k - 8)

    def x_right(s):
        ref = slot(0, NZ - s)
        return remote(ref, ref, zr_s.at[s], zr_r.at[s], right)

    def x_left(s):
        ref = slot(0, s)
        return remote(ref, ref, zl_s.at[s], zl_r.at[s], left)

    def x_up(k):
        ref = slot(0, z_of(k))
        return remote(ref, ref, yp_s.at[k], yp_r.at[k], dev(1, 0))

    def x_down(k):
        ref = slot(0, z_of(k))
        return remote(ref, ref, ym_s.at[k], ym_r.at[k], dev(3, 0))

    def x_pass_up(k):
        ref = slot(3, z_of(k)).at[pl.ds(0, rows // 2)]
        return remote(ref, ref, fp_s.at[k], fp_r.at[k], dev(1, 0))

    def x_pass_down(k):
        ref = slot(1, z_of(k)).at[pl.ds(rows // 2, rows // 2)]
        return remote(ref, ref, fm_s.at[k], fm_r.at[k], dev(3, 0))

    def x_pass(k):
        x_up(k).wait_recv()
        x_pass_up(k).start()
        x_down(k).wait_recv()
        x_pass_down(k).start()

    def cells(g):
        return pl.ds(g * WIDE, WIDE)

    def go_right(j, g):
        src = first.at[cells(g)] if j == 0 else rbuf.at[j - 1, cells(g)]
        return remote(src, rbuf.at[j, cells(g)], r_s.at[j, g], r_r.at[j, g], right)

    def go_left(j, g):
        src = first.at[cells(g)] if j == 0 else lbuf.at[j - 1, cells(g)]
        return remote(src, lbuf.at[j, cells(g)], l_s.at[j, g], l_r.at[j, g], left)

    def wait_y(far):
        for dy in range(1, NY):
            over_y(far, dy).wait_recv()

    def columns(far):
        there = (z + far) % NZ
        return [[cols_ref[there // 2, (y + NY - dy) % NY, child] for child in range(2)] for dy in range(NY)]

    def items(total, cols, far, cell):
        for dy in range(NY):
            for child in range(2):
                share = (cols[dy][child] == cell).astype(jnp.float32)
                tile = packed[far, y, child] if dy == 0 else ybuf[far, dy - 1, child]
                total = total + share * tile
        return total

    def merge(buf, fresh, cols, far, g):
        def one(n, carry):
            cell = g * WIDE + n
            start = jnp.zeros(buf.shape[1:], jnp.float32) if fresh else buf[cell]
            buf[cell] = items(start, cols, far, cell)
            return carry

        lax.fori_loop(0, WIDE, one, 0)

    half_chunks = CHUNKS // 2
    x_right(0).start()
    x_left(0).start()
    wait_y(8)
    cols = columns(8)
    for g in range(CHUNKS):
        merge(first, True, cols, 8, g)
        (go_right(0, g) if g < half_chunks else go_left(0, g)).start()
    x_up(0).start()
    x_down(0).start()

    behind = [0]
    for j in range(1, 9):
        far_r, far_l = 8 - j, (8 + j) % NZ
        wait_y(far_r)
        if j < 8:
            wait_y(far_l)
            cols_r, cols_l = columns(far_r), columns(far_l)
            for g in range(CHUNKS):
                fresh = j == 1 and g >= half_chunks
                if not fresh:
                    go_right(j - 1, g).wait_recv()
                merge(rbuf.at[j - 1], fresh, cols_r, far_r, g)
                go_right(j, g).start()
                fresh = j == 1 and g < half_chunks
                if not fresh:
                    go_left(j - 1, g).wait_recv()
                merge(lbuf.at[j - 1], fresh, cols_l, far_l, g)
                go_left(j, g).start()
        x_right(j - 1).wait_recv()
        if j < 8:
            x_right(j).start()
            x_left(j - 1).wait_recv()
            if j < 7:
                x_left(j).start()
        x_up(j).start()
        x_down(j).start()
        if j < 8:
            x_up(j + 8).start()
            x_down(j + 8).start()
        for k in behind:
            x_pass(k)
        behind = [j] if j == 8 else [j, j + 8]

    cols = columns(0)
    for g in range(CHUNKS):
        go_right(7, g).wait_recv()
        go_left(7, g).wait_recv()
        for n in range(WIDE):
            cell = g * WIDE + n
            t_ref[:, cell * 128:(cell + 1) * 128] = items(rbuf[7, cell] + lbuf[7, cell], cols, 0, cell)
    for k in behind:
        x_pass(k)

    for k in range(NZ):
        x_pass_up(k).wait_recv()
        x_pass_down(k).wait_recv()
        for copy in (x_up(k), x_down(k), x_pass_up(k), x_pass_down(k)):
            copy.wait_send()
        for dy in range(1, NY):
            over_y(k, dy).wait_send()
    for s in range(8):
        x_right(s).wait_send()
        if s < 7:
            x_left(s).wait_send()
    for j in range(8):
        for g in range(CHUNKS):
            if j > 0 or g < half_chunks:
                go_right(j, g).wait_send()
            if j > 0 or g >= half_chunks:
                go_left(j, g).wait_send()


def exchange(front, own_tiles, partner_tiles, pick, cols, lead):
    rows = front.shape[1]
    tile = own_tiles.shape[-1]
    slots = own_tiles.shape[1]
    sem = pltpu.SemaphoreType.DMA
    any_spec = pl.BlockSpec(memory_space=pl.ANY)
    smem = pl.BlockSpec(memory_space=pltpu.SMEM)
    f32 = jnp.float32
    return pl.pallas_call(
        exchange_kernel,
        out_shape=(
            jax.ShapeDtypeStruct((NY * NZ, rows, lead), f32),
            jax.ShapeDtypeStruct((rows, CELLS * tile), f32),
        ),
        in_specs=[any_spec, any_spec, any_spec, smem, smem],
        out_specs=(any_spec, pl.BlockSpec(memory_space=pltpu.VMEM)),
        scratch_shapes=[
            pltpu.VMEM((2 * slots + 1, tile, tile), f32),
            pltpu.VMEM((NZ, NY, 2, rows, tile), f32),
            pltpu.VMEM((NZ, NY - 1, 2, rows, tile), f32),
            pltpu.VMEM((8, CELLS, rows, tile), f32),
            pltpu.VMEM((8, CELLS, rows, tile), f32),
            pltpu.VMEM((CELLS, rows, tile), f32),
            sem((2,)), sem, sem,
            sem((NZ, NY - 1)), sem((NZ, NY - 1)),
            sem((8, CHUNKS)), sem((8, CHUNKS)), sem((8, CHUNKS)), sem((8, CHUNKS)),
            sem((8,)), sem((8,)), sem((7,)), sem((7,)),
        ] + [sem((NZ,))] * 8,
        compiler_params=pltpu.CompilerParams(
            collective_id=0, has_side_effects=True, vmem_limit_bytes=48 * 2**20
        ),
    )(front, own_tiles, partner_tiles, pick, cols)


def factor(lead):
    order = lead.shape[0]
    row = lax.broadcasted_iota(jnp.int32, (order, order), 0)
    col = lax.broadcasted_iota(jnp.int32, (order, order), 1)
    unit = (row == col).astype(jnp.float32)
    keep = jnp.where(row > col, 1.0, jnp.where(row == col, 0.5, 0.0))
    scale = lax.rsqrt(jnp.sum(lead * unit, axis=1))
    gap = lead * scale[:, None] * scale[None, :] - unit
    inverse = (unit - keep * gap) * scale[None, :]
    for _ in range(ROUNDS - 1):
        gap = jnp.dot(jnp.dot(inverse, lead, precision=HIGH), inverse.T, precision=HIGH) - unit
        inverse = inverse - jnp.dot(keep * gap, inverse, precision=HIGH)
    return inverse


def body(front, own_tiles, partner_tiles, tile_rows, tile_cols, live):
    position = lax.axis_index("cube")
    front_pos = lax.axis_index("front")
    rows_dev = front.shape[1]
    order_size = front.shape[2]
    tile = own_tiles.shape[-1]
    slots = own_tiles.shape[1]
    tile_count = order_size // tile
    lead = PANELS * tile
    y, z = position // NZ, position % NZ

    rows_here = lax.dynamic_index_in_dim(tile_rows, front_pos, 0, keepdims=False)[:, :, 0]
    cols_here = lax.dynamic_index_in_dim(tile_cols, front_pos, 0, keepdims=False)
    live_here = lax.dynamic_index_in_dim(live, front_pos, 0, keepdims=False)
    within = jnp.arange(slots)
    rows_z = lax.dynamic_slice_in_dim(rows_here.reshape(NY, NZ, 2, slots), z, 1, 1)[:, 0]
    cols_z = lax.dynamic_slice_in_dim(cols_here.reshape(NY, NZ, 2, slots), z, 1, 1)[:, 0]
    live_z = lax.dynamic_slice_in_dim(live_here.reshape(NY, NZ, 2), z, 1, 1)[:, 0]
    rows_z = jnp.where(within < live_z[:, :, None], rows_z, -1)
    rows_mine = lax.dynamic_index_in_dim(rows_z, y, 0, keepdims=False)
    hit = rows_mine[:, :, None] == jnp.arange(tile_count)
    spot = within[None, :] + slots * jnp.arange(2)[:, None] - 2 * slots
    pick = jnp.sum(jnp.where(hit, spot[:, :, None], 0), axis=1) + 2 * slots
    hit = rows_z[None] == (y * (NZ // 2) + jnp.arange(NZ // 2))[:, None, None, None]
    cols = jnp.sum(jnp.where(hit, cols_z - (PANELS - 1), 0), axis=3) - 1

    panels, added = exchange(front, own_tiles, partner_tiles, pick, cols, lead)
    panels = panels.reshape(order_size, lead)
    own_panel = front[0, :, :lead]
    inverse = factor(panels[:lead])
    row_global = position * rows_dev + jnp.arange(rows_dev)[:, None]
    col_global = jnp.arange(lead)[None, :]
    own_factor = jnp.dot(own_panel, inverse.T, precision=HIGH)
    own_factor = jnp.where(col_global <= row_global, own_factor, 0.0)
    earlier = jnp.where(col_global < row_global // tile * tile, own_factor, 0.0)
    weights = jnp.dot(earlier, inverse, precision=HIGH)
    product = jnp.dot(weights, panels[lead:].T, precision=HIGH)
    rest = front[0, :, lead:] - product + added
    return jnp.concatenate([own_factor, rest], axis=1)[None]


def solution(mesh):
    in_specs = (
        P("front", "cube", None),
        P("front", "cube", None, None),
        P("front", "cube", None, None),
        P(),
        P(),
        P(),
    )
    out_specs = P("front", "cube", None)
    return jax.shard_map(body, mesh=mesh, in_specs=in_specs, out_specs=out_specs, check_vma=False)
```

```python
import jax
import jax.numpy as jnp
from jax import lax
from jax.experimental import pallas as pl
from jax.experimental.pallas import tpu as pltpu
from jax.sharding import PartitionSpec as P

PANELS = 4
NY = 4
NZ = 16
CELLS = 28
CHUNKS = 4
WIDE = CELLS // CHUNKS
ROUNDS = 6
SUB = 128
MESH = pl.DeviceIdType.MESH
NN = (((1,), (0,)), ((), ()))
NT = (((1,), (1,)), ((), ()))


def split(value):
    high = value.astype(jnp.bfloat16)
    return high, (value - high.astype(jnp.float32)).astype(jnp.bfloat16)


def dot3(left, right, dims):
    def dot(a, b):
        return lax.dot_general(a, b, dims, preferred_element_type=jnp.float32)

    return dot(left[0], right[1]) + dot(left[1], right[0]) + dot(left[0], right[0])


def exchange_kernel(
    front_ref, own_ref, partner_ref, pick_ref, cols_ref, out_ref,
    tiles, packed, ybuf, raw1, raw2, raw3, dense, xbuf,
    lead_ref, m_ref, t_ref, g_ref, a_hi, a_lo, m_hi, m_lo, w_hi, w_lo,
    load_sem, pair_s, pair_r, y_s, y_r, raw_s, raw_r, d_s, d_r,
    zr_s, zr_r, zl_s, zl_r, yp_s, yp_r, ym_s, ym_r, fp_s, fp_r, fm_s, fm_r,
):
    me = lax.axis_index("cube")
    side = lax.axis_index("front")
    y, z = me // NZ, me % NZ
    rows, lead = xbuf.shape[1], xbuf.shape[2]
    slots = own_ref.shape[1]
    none = 2 * slots
    tile = tiles.shape[1]

    def dev(dy, dz):
        return {"cube": (y + dy) % NY * NZ + (z + dz) % NZ}

    mate = {"front": side + 1 - 2 * (side % 2)}
    toward = [dev(0, 1), dev(0, NZ - 1)]
    peers = toward + [dev(1, 0), dev(2, 0), dev(3, 0), mate]
    barrier = pltpu.get_barrier_semaphore()
    for peer in peers:
        pl.semaphore_signal(barrier, inc=1, device_id=peer, device_id_type=MESH)
    xbuf[me] = front_ref[0, :, :lead]
    pl.semaphore_wait(barrier, len(peers))

    def remote(src, dst, send, recv, to):
        return pltpu.make_async_remote_copy(
            src_ref=src, dst_ref=dst, send_sem=send, recv_sem=recv, device_id=to, device_id_type=MESH
        )

    pair = remote(partner_ref.at[0], tiles.at[pl.ds(slots, slots)], pair_s, pair_r, mate)
    pair.start()
    own = pltpu.make_async_copy(own_ref.at[0], tiles.at[pl.ds(0, slots)], load_sem)
    own.start()

    def z_abs(k):
        return (z + (0 if k == 0 else (NZ - k if k <= 8 else k - 8))) % NZ

    def slot(dy, zz):
        return xbuf.at[(y + dy) % NY * NZ + zz]

    def x_right(s):
        ref = slot(0, (z + NZ - s) % NZ)
        return remote(ref, ref, zr_s.at[s], zr_r.at[s], toward[0])

    def x_left(s):
        ref = slot(0, (z + s) % NZ)
        return remote(ref, ref, zl_s.at[s], zl_r.at[s], toward[1])

    def x_up(zz):
        ref = slot(0, zz)
        return remote(ref, ref, yp_s.at[zz], yp_r.at[zz], dev(1, 0))

    def x_down(zz):
        ref = slot(0, zz)
        return remote(ref, ref, ym_s.at[zz], ym_r.at[zz], dev(3, 0))

    def x_pass_up(zz):
        ref = slot(3, zz).at[pl.ds(0, rows // 2)]
        return remote(ref, ref, fp_s.at[zz], fp_r.at[zz], dev(1, 0))

    def x_pass_down(zz):
        ref = slot(1, zz).at[pl.ds(rows // 2, rows // 2)]
        return remote(ref, ref, fm_s.at[zz], fm_r.at[zz], dev(3, 0))

    def x_out(k):
        x_up(z_abs(k)).start()
        x_down(z_abs(k)).start()

    def x_pass(k):
        zz = z_abs(k)
        x_up(zz).wait_recv()
        x_pass_up(zz).start()
        x_down(zz).wait_recv()
        x_pass_down(zz).start()

    behind = [0]

    def x_step(s):
        x_right(s - 1).wait_recv()
        if s < 8:
            x_right(s).start()
            x_left(s - 1).wait_recv()
            if s < 7:
                x_left(s).start()
        now = [s] if s == 8 else [s, s + 8]
        for k in now:
            x_out(k)
        for k in behind:
            x_pass(k)
        behind[:] = now

    x_right(0).start()
    x_left(0).start()
    x_out(0)
    tiles[none] = jnp.zeros(tiles.shape[1:], jnp.float32)
    own.wait()
    pair.wait()

    def over_y(far, dy):
        return remote(
            packed.at[far, (y + dy) % NY], ybuf.at[far, pl.ds(2 * dy - 2, 2)],
            y_s.at[far, dy - 1], y_r.at[far, dy - 1], dev(dy, 0),
        )

    def pack(far):
        there = (z + far) % NZ
        top = pl.multiple_of(there % 2 * rows, rows)
        for to_y in range(NY):
            for child in range(2):
                index = pick_ref[child, to_y * (NZ // 2) + there // 2]
                packed[far, to_y, child] = tiles[index, pl.ds(top, rows), :]
        for dy in range(1, NY):
            over_y(far, dy).start()

    def wait_y(far):
        for dy in range(1, NY):
            over_y(far, dy).wait_recv()

    def far_of(way, j):
        return (8 - j if way == 0 else 8 + j) % NZ

    half_list = 4

    def raw_go(way, j):
        far = far_of(way, j)
        to = toward[way]
        dst = (raw1, raw2, raw3)[j]
        mine = packed.at[far, y]
        theirs = ybuf.at[far]
        if j == 0:
            if way == 0:
                pairs = [(mine, pl.ds(0, 2)), (theirs.at[pl.ds(0, 2)], pl.ds(2, 2))]
            else:
                pairs = [(theirs.at[pl.ds(2, 4)], pl.ds(0, 4))]
        else:
            before = (raw1, raw2)[j - 1]
            count = before.shape[1]
            pairs = [(mine, pl.ds(0, 2)), (theirs, pl.ds(2, 6)), (before.at[way], pl.ds(8, count))]
        return [
            remote(a, dst.at[way, b], raw_s.at[way, j, n], raw_r.at[way, j, n], to)
            for n, (a, b) in enumerate(pairs)
        ]

    def cells(g):
        return pl.ds(g * WIDE, WIDE)

    def go(way, j, g):
        return remote(
            dense.at[way, j - 3, cells(g)], dense.at[way, j - 2, cells(g)],
            d_s.at[way, j - 3, g], d_r.at[way, j - 3, g], toward[way],
        )

    def list_cols(far_dest, dz, members):
        there = (z + far_dest) % NZ
        at = (z + dz) % NZ * (NZ // 2) + there // 2
        return [cols_ref[at, (y + NY - dy) % NY * 2 + child] for dy, child in members]

    full = [(dy, child) for dy in range(NY) for child in range(2)]

    def own_items(far):
        cols = list_cols(far, 0, full)
        refs = [packed.at[far, y, c] if dy == 0 else ybuf.at[far, 2 * dy - 2 + c] for dy, c in full]
        return list(zip(cols, refs))

    def raw_items(way, far):
        step = NZ - 1 if way == 0 else 1
        last = full[:half_list] if way == 0 else full[half_list:]
        cols = list_cols(far, step, full) + list_cols(far, 2 * step, full) + list_cols(far, 3 * step, last)
        return [(col, raw3.at[way, n]) for n, col in enumerate(cols)]

    def add(total, items, cell):
        for col, ref in items:
            total = total + (col == cell).astype(jnp.float32) * ref[...]
        return total

    def merge(buf, fresh, items, g):
        def one(n, carry):
            cell = g * WIDE + n
            start = jnp.zeros(buf.shape[1:], jnp.float32) if fresh else buf[cell]
            buf[cell] = add(start, items, cell)
            return carry

        lax.fori_loop(0, WIDE, one, 0)

    def strip(body):
        def one(n, carry):
            body(pl.ds(pl.multiple_of(n * SUB, SUB), SUB), n * SUB)
            return carry

        lax.fori_loop(0, lead // SUB, one, 0)

    def places(start, shape):
        row = lax.broadcasted_iota(jnp.int32, shape, 0) + start
        col = lax.broadcasted_iota(jnp.int32, shape, 1)
        return row, col

    def load_lead():
        for zz in range(8):
            x_pass_up(zz).wait_recv()
            x_pass_down(zz).wait_recv()

        def rows_of(at, start):
            block = xbuf[pl.ds(start // rows, SUB // rows)].reshape(SUB, lead)
            lead_ref[at, :] = block
            a_hi[at, :], a_lo[at, :] = split(block)

        strip(rows_of)

    def keep_m(at, value):
        m_ref[at, :] = value
        m_hi[at, :], m_lo[at, :] = split(value)

    def begin():
        def diagonal(at, start):
            row, col = places(start, (SUB, lead))
            t_ref[at, :] = jnp.where(row == col, lead_ref[at, :], 0.0)

        strip(diagonal)
        across = lax.rsqrt(jnp.sum(t_ref[...], axis=0, keepdims=True))

        def rows_of(at, start):
            row, col = places(start, (SUB, lead))
            down = lax.rsqrt(jnp.sum(t_ref[at, :], axis=1, keepdims=True))
            lower = jnp.where(row > col, lead_ref[at, :] * down, 0.0)
            unit = (row == col).astype(jnp.float32)
            diag = jnp.where(row == col, lead_ref[at, :], 0.0) * down * across
            keep_m(at, (unit - lower * across - 0.5 * (diag - unit)) * across)

        strip(rows_of)

    def round_a():
        def rows_of(at, start):
            t_ref[at, :] = dot3((m_hi[at, :], m_lo[at, :]), (a_hi[...], a_lo[...]), NN)

        strip(rows_of)

    def round_b():
        def rows_of(at, start):
            row, col = places(start, (SUB, lead))
            gap = dot3(split(t_ref[at, :]), (m_hi[...], m_lo[...]), NT)
            g_ref[at, :] = jnp.where(row > col, gap, jnp.where(row == col, 0.5 * (gap - 1.0), 0.0))

        strip(rows_of)

    def round_c():
        def rows_of(at, start):
            t_ref[at, :] = m_ref[at, :] - dot3(split(g_ref[at, :]), (m_hi[...], m_lo[...]), NN)

        strip(rows_of)
        strip(lambda at, start: keep_m(at, t_ref[at, :]))

    def weigh():
        inverse = (m_hi[...], m_lo[...])
        row, col = places(me * rows, (rows, lead))
        value = dot3(split(xbuf[me]), inverse, NT)
        value = jnp.where(col <= row, value, 0.0)
        out_ref[0, :, :lead] = value
        value = jnp.where(col < row // tile * tile, value, 0.0)
        w_hi[...], w_lo[...] = split(dot3(split(value), inverse, NN))

    def rest_panels():
        for zz in range(8, NZ):
            x_pass_up(zz).wait_recv()
            x_pass_down(zz).wait_recv()

    def subtract(g):
        weights = (w_hi[...], w_lo[...])

        def one(n, carry):
            cell = g * WIDE + n
            block = xbuf[pl.ds(lead // rows + tile // rows * cell, tile // rows)].reshape(tile, lead)
            at = pl.ds(pl.multiple_of(lead + cell * tile, tile), tile)
            out_ref[0, :, at] = front_ref[0, :, at] - dot3(weights, split(block), NT)
            return carry

        lax.fori_loop(0, WIDE, one, 0)

    todo = [load_lead, begin]
    for _ in range(ROUNDS - 1):
        todo += [round_a, round_b, round_c]
    todo += [weigh, rest_panels] + [lambda g=g: subtract(g) for g in range(CHUNKS)]

    def work(count):
        for _ in range(count):
            if todo:
                todo.pop(0)()

    for far in (8, 7, 9, 6, 10):
        pack(far)
    x_step(1)
    wait_y(8)
    for way in range(2):
        for copy in raw_go(way, 0):
            copy.start()
    for j in range(1, 3):
        x_step(2 * j)
        for way in range(2):
            wait_y(far_of(way, j))
            for copy in raw_go(way, j - 1):
                copy.wait_recv()
            for copy in raw_go(way, j):
                copy.start()
        pack(far_of(0, j + 2))
        pack(far_of(1, j + 2))
        x_step(2 * j + 1)
    for way in range(2):
        wait_y(far_of(way, 3))
        for copy in raw_go(way, 2):
            copy.wait_recv()
    items = [own_items(far_of(way, 3)) + raw_items(way, far_of(way, 3)) for way in range(2)]
    for g in range(CHUNKS):
        for way in range(2):
            merge(dense.at[way, 0], True, items[way], g)
            go(way, 3, g).start()
    for far in (far_of(0, 5), far_of(1, 5), far_of(0, 6), far_of(1, 6)):
        pack(far)
    x_step(6)
    x_step(7)
    for j in range(4, 8):
        for way in range(2):
            wait_y(far_of(way, j))
        items = [own_items(far_of(way, j)) for way in range(2)]
        for g in range(CHUNKS):
            for way in range(2):
                go(way, j - 1, g).wait_recv()
                merge(dense.at[way, j - 3], False, items[way], g)
                go(way, j, g).start()
            if j > 4:
                work(2)
        if j == 4:
            for far in (far_of(0, 7), far_of(1, 7), 0):
                pack(far)
            x_step(8)
            for k in behind:
                x_pass(k)

    while todo:
        work(1)
    wait_y(0)
    items = own_items(0)
    for g in range(CHUNKS):
        for way in range(2):
            go(way, 7, g).wait_recv()

        def last(n, carry):
            cell = g * WIDE + n
            at = pl.ds(pl.multiple_of(lead + cell * tile, tile), tile)
            total = add(dense[0, 5, cell] + dense[1, 5, cell], items, cell)
            out_ref[0, :, at] = out_ref[0, :, at] + total
            return carry

        lax.fori_loop(0, WIDE, last, 0)

    for zz in range(NZ):
        for copy in (x_up(zz), x_down(zz), x_pass_up(zz), x_pass_down(zz)):
            copy.wait_send()
        for dy in range(1, NY):
            over_y(zz, dy).wait_send()
    for s in range(8):
        x_right(s).wait_send()
        if s < 7:
            x_left(s).wait_send()
    for way in range(2):
        for j in range(3):
            for copy in raw_go(way, j):
                copy.wait_send()
        for j in range(3, 8):
            for g in range(CHUNKS):
                go(way, j, g).wait_send()


def exchange(front, own_tiles, partner_tiles, pick, cols, lead):
    rows = front.shape[1]
    tile = own_tiles.shape[-1]
    slots = own_tiles.shape[1]
    sem = pltpu.SemaphoreType.DMA
    any_spec = pl.BlockSpec(memory_space=pl.ANY)
    smem = pl.BlockSpec(memory_space=pltpu.SMEM)
    vmem = pl.BlockSpec(memory_space=pltpu.VMEM)
    f32, bf16 = jnp.float32, jnp.bfloat16
    return pl.pallas_call(
        exchange_kernel,
        out_shape=jax.ShapeDtypeStruct(front.shape, f32),
        in_specs=[vmem, any_spec, any_spec, smem, smem],
        out_specs=vmem,
        scratch_shapes=[
            pltpu.VMEM((2 * slots + 1, tile, tile), f32),
            pltpu.VMEM((NZ, NY, 2, rows, tile), f32),
            pltpu.VMEM((NZ, 2 * NY - 2, rows, tile), f32),
            pltpu.VMEM((2, 4, rows, tile), f32),
            pltpu.VMEM((2, 12, rows, tile), f32),
            pltpu.VMEM((2, 20, rows, tile), f32),
            pltpu.VMEM((2, 6, CELLS, rows, tile), f32),
            pltpu.VMEM((NY * NZ, rows, lead), f32),
        ]
        + [pltpu.VMEM((lead, lead), f32)] * 4
        + [pltpu.VMEM((lead, lead), bf16)] * 4
        + [pltpu.VMEM((rows, lead), bf16)] * 2
        + [
            sem, sem, sem,
            sem((NZ, NY - 1)), sem((NZ, NY - 1)),
            sem((2, 3, 3)), sem((2, 3, 3)),
            sem((2, 5, CHUNKS)), sem((2, 5, CHUNKS)),
            sem((8,)), sem((8,)), sem((7,)), sem((7,)),
        ] + [sem((NZ,))] * 8,
        compiler_params=pltpu.CompilerParams(
            collective_id=0, has_side_effects=True, vmem_limit_bytes=56 * 2**20
        ),
    )(front, own_tiles, partner_tiles, pick, cols)


def body(front, own_tiles, partner_tiles, tile_rows, tile_cols, live):
    position = lax.axis_index("cube")
    front_pos = lax.axis_index("front")
    tile = own_tiles.shape[-1]
    slots = own_tiles.shape[1]
    tile_count = front.shape[2] // tile
    y, z = position // NZ, position % NZ

    rows_here = lax.dynamic_index_in_dim(tile_rows, front_pos, 0, keepdims=False)[:, :, 0]
    cols_here = lax.dynamic_index_in_dim(tile_cols, front_pos, 0, keepdims=False)
    live_here = lax.dynamic_index_in_dim(live, front_pos, 0, keepdims=False)
    within = jnp.arange(slots)
    rows_here = rows_here.reshape(NY * NZ, 2, slots)
    cols_here = cols_here.reshape(NY * NZ, 2, slots)
    rows_here = jnp.where(within < live_here[:, :, None], rows_here, -1)
    rows_mine = lax.dynamic_index_in_dim(rows_here, position, 0, keepdims=False)
    hit = rows_mine[:, :, None] == jnp.arange(tile_count)
    spot = within[None, :] + slots * jnp.arange(2)[:, None] - 2 * slots
    pick = jnp.sum(jnp.where(hit, spot[:, :, None], 0), axis=1) + 2 * slots
    hit = rows_here[None] == (y * (NZ // 2) + jnp.arange(NZ // 2))[:, None, None, None]
    cols = jnp.sum(jnp.where(hit, cols_here - (PANELS - 1), 0), axis=3) - 1
    cols = cols.reshape(NZ // 2, NY, NZ, 2).transpose(2, 0, 1, 3).reshape(NZ * NZ // 2, 2 * NY)
    return exchange(front, own_tiles, partner_tiles, pick, cols, PANELS * tile)


def solution(mesh):
    in_specs = (
        P("front", "cube", None),
        P("front", "cube", None, None),
        P("front", "cube", None, None),
        P(),
        P(),
        P(),
    )
    out_specs = P("front", "cube", None)
    return jax.shard_map(body, mesh=mesh, in_specs=in_specs, out_specs=out_specs, check_vma=False)
```

```python
import jax
import jax.numpy as jnp
from jax import lax
from jax.experimental import pallas as pl
from jax.experimental.pallas import tpu as pltpu
from jax.sharding import PartitionSpec as P

PANELS = 4
NY = 4
NZ = 16
CELLS = 28
CHUNKS = 4
WIDE = CELLS // CHUNKS
ROUNDS = 6
SUB = 128
MESH = pl.DeviceIdType.MESH
NN = (((1,), (0,)), ((), ()))
NT = (((1,), (1,)), ((), ()))


def split(value):
    high = value.astype(jnp.bfloat16)
    return high, (value - high.astype(jnp.float32)).astype(jnp.bfloat16)


def dot3(left, right, dims):
    def dot(a, b):
        return lax.dot_general(a, b, dims, preferred_element_type=jnp.float32)

    return dot(left[0], right[1]) + dot(left[1], right[0]) + dot(left[0], right[0])


def exchange_kernel(
    front_ref, own_ref, partner_ref, pick_ref, cols_ref, out_ref,
    tiles, packed, ybuf, raw1, raw2, raw3, dense, xbuf,
    lead_ref, m_ref, t_ref, g_ref, a_hi, a_lo, m_hi, m_lo, w_hi, w_lo,
    load_sem, pair_s, pair_r, y_s, y_r, raw_s, raw_r, d_s, d_r,
    zr_s, zr_r, zl_s, zl_r, yp_s, yp_r, ym_s, ym_r, fp_s, fp_r, fm_s, fm_r,
):
    me = lax.axis_index("cube")
    side = lax.axis_index("front")
    y, z = me // NZ, me % NZ
    rows, lead = xbuf.shape[1], xbuf.shape[2]
    slots = own_ref.shape[1]
    none = 2 * slots
    tile = tiles.shape[1]

    def dev(dy, dz):
        return {"cube": (y + dy) % NY * NZ + (z + dz) % NZ}

    mate = {"front": side + 1 - 2 * (side % 2)}
    toward = [dev(0, 1), dev(0, NZ - 1)]
    peers = toward + [dev(1, 0), dev(2, 0), dev(3, 0), mate]
    barrier = pltpu.get_barrier_semaphore()
    for peer in peers:
        pl.semaphore_signal(barrier, inc=1, device_id=peer, device_id_type=MESH)
    xbuf[me] = front_ref[0, :, :lead]
    pl.semaphore_wait(barrier, len(peers))

    def remote(src, dst, send, recv, to):
        return pltpu.make_async_remote_copy(
            src_ref=src, dst_ref=dst, send_sem=send, recv_sem=recv, device_id=to, device_id_type=MESH
        )

    pair = remote(partner_ref.at[0], tiles.at[pl.ds(slots, slots)], pair_s, pair_r, mate)
    pair.start()
    own = pltpu.make_async_copy(own_ref.at[0], tiles.at[pl.ds(0, slots)], load_sem)
    own.start()

    def slot(dy, zz):
        return xbuf.at[(y + dy) % NY * NZ + zz]

    def x_right(s):
        ref = slot(0, (z + NZ - s) % NZ)
        return remote(ref, ref, zr_s.at[s], zr_r.at[s], toward[0])

    def x_left(s):
        ref = slot(0, (z + s) % NZ)
        return remote(ref, ref, zl_s.at[s], zl_r.at[s], toward[1])

    def x_up(zz):
        ref = slot(0, zz)
        return remote(ref, ref, yp_s.at[zz], yp_r.at[zz], dev(1, 0))

    def x_down(zz):
        ref = slot(0, zz)
        return remote(ref, ref, ym_s.at[zz], ym_r.at[zz], dev(3, 0))

    def x_pass_up(zz):
        ref = slot(3, zz).at[pl.ds(0, rows // 2)]
        return remote(ref, ref, fp_s.at[zz], fp_r.at[zz], dev(1, 0))

    def x_pass_down(zz):
        ref = slot(1, zz).at[pl.ds(rows // 2, rows // 2)]
        return remote(ref, ref, fm_s.at[zz], fm_r.at[zz], dev(3, 0))

    def x_out(zz):
        x_up(zz).start()
        x_down(zz).start()

    def x_pass(zz):
        x_up(zz).wait_recv()
        x_pass_up(zz).start()
        x_down(zz).wait_recv()
        x_pass_down(zz).start()

    def x_step(s):
        x_right(s - 1).wait_recv()
        if s < 8:
            x_right(s).start()
            x_left(s - 1).wait_recv()
            if s < 7:
                x_left(s).start()

    x_right(0).start()
    x_left(0).start()
    tiles[none] = jnp.zeros(tiles.shape[1:], jnp.float32)
    own.wait()
    pair.wait()

    def over_y(far, dy):
        return remote(
            packed.at[far, (y + dy) % NY], ybuf.at[far, pl.ds(2 * dy - 2, 2)],
            y_s.at[far, dy - 1], y_r.at[far, dy - 1], dev(dy, 0),
        )

    def pack(far):
        there = (z + far) % NZ
        top = pl.multiple_of(there % 2 * rows, rows)
        for to_y in range(NY):
            for child in range(2):
                index = pick_ref[child, to_y * (NZ // 2) + there // 2]
                packed[far, to_y, child] = tiles[index, pl.ds(top, rows), :]
        for dy in range(1, NY):
            over_y(far, dy).start()

    def wait_y(far):
        for dy in range(1, NY):
            over_y(far, dy).wait_recv()

    def far_of(way, j):
        return (8 - j if way == 0 else 8 + j) % NZ

    half_list = 4

    def raw_go(way, j):
        far = far_of(way, j)
        to = toward[way]
        dst = (raw1, raw2, raw3)[j]
        mine = packed.at[far, y]
        theirs = ybuf.at[far]
        if j == 0:
            if way == 0:
                pairs = [(mine, pl.ds(0, 2)), (theirs.at[pl.ds(0, 2)], pl.ds(2, 2))]
            else:
                pairs = [(theirs.at[pl.ds(2, 4)], pl.ds(0, 4))]
        else:
            before = (raw1, raw2)[j - 1]
            count = before.shape[1]
            pairs = [(mine, pl.ds(0, 2)), (theirs, pl.ds(2, 6)), (before.at[way], pl.ds(8, count))]
        return [
            remote(a, dst.at[way, b], raw_s.at[way, j, n], raw_r.at[way, j, n], to)
            for n, (a, b) in enumerate(pairs)
        ]

    def cells(g):
        return pl.ds(g * WIDE, WIDE)

    def go(way, j, g):
        return remote(
            dense.at[way, j - 3, cells(g)], dense.at[way, j - 2, cells(g)],
            d_s.at[way, j - 3, g], d_r.at[way, j - 3, g], toward[way],
        )

    def list_cols(far_dest, dz, members):
        there = (z + far_dest) % NZ
        at = (z + dz) % NZ * (NZ // 2) + there // 2
        return [cols_ref[at, (y + NY - dy) % NY * 2 + child] for dy, child in members]

    full = [(dy, child) for dy in range(NY) for child in range(2)]

    def own_items(far):
        cols = list_cols(far, 0, full)
        refs = [packed.at[far, y, c] if dy == 0 else ybuf.at[far, 2 * dy - 2 + c] for dy, c in full]
        return list(zip(cols, refs))

    def raw_items(way, far):
        step = NZ - 1 if way == 0 else 1
        last = full[:half_list] if way == 0 else full[half_list:]
        cols = list_cols(far, step, full) + list_cols(far, 2 * step, full) + list_cols(far, 3 * step, last)
        return [(col, raw3.at[way, n]) for n, col in enumerate(cols)]

    def add(total, items, cell):
        for col, ref in items:
            total = total + (col == cell).astype(jnp.float32) * ref[...]
        return total

    def merge(buf, fresh, items, g):
        def one(n, carry):
            cell = g * WIDE + n
            start = jnp.zeros(buf.shape[1:], jnp.float32) if fresh else buf[cell]
            buf[cell] = add(start, items, cell)
            return carry

        lax.fori_loop(0, WIDE, one, 0)

    def strip(body):
        def one(n, carry):
            body(pl.ds(pl.multiple_of(n * SUB, SUB), SUB), n * SUB)
            return carry

        lax.fori_loop(0, lead // SUB, one, 0)

    def places(start, shape):
        row = lax.broadcasted_iota(jnp.int32, shape, 0) + start
        col = lax.broadcasted_iota(jnp.int32, shape, 1)
        return row, col

    def load_lead():
        for zz in range(8):
            x_pass_up(zz).wait_recv()
            x_pass_down(zz).wait_recv()

        def rows_of(at, start):
            block = xbuf[pl.ds(start // rows, SUB // rows)].reshape(SUB, lead)
            lead_ref[at, :] = block
            a_hi[at, :], a_lo[at, :] = split(block)

        strip(rows_of)

    def keep_m(at, value):
        m_ref[at, :] = value
        m_hi[at, :], m_lo[at, :] = split(value)

    def begin():
        def diagonal(at, start):
            row, col = places(start, (SUB, lead))
            t_ref[at, :] = jnp.where(row == col, lead_ref[at, :], 0.0)

        strip(diagonal)
        across = lax.rsqrt(jnp.sum(t_ref[...], axis=0, keepdims=True))

        def rows_of(at, start):
            row, col = places(start, (SUB, lead))
            down = lax.rsqrt(jnp.sum(t_ref[at, :], axis=1, keepdims=True))
            lower = jnp.where(row > col, lead_ref[at, :] * down, 0.0)
            unit = (row == col).astype(jnp.float32)
            diag = jnp.where(row == col, lead_ref[at, :], 0.0) * down * across
            keep_m(at, (unit - lower * across - 0.5 * (diag - unit)) * across)

        strip(rows_of)

    def round_a():
        def rows_of(at, start):
            t_ref[at, :] = dot3((m_hi[at, :], m_lo[at, :]), (a_hi[...], a_lo[...]), NN)

        strip(rows_of)

    def round_b():
        def rows_of(at, start):
            row, col = places(start, (SUB, lead))
            gap = dot3(split(t_ref[at, :]), (m_hi[...], m_lo[...]), NT)
            g_ref[at, :] = jnp.where(row > col, gap, jnp.where(row == col, 0.5 * (gap - 1.0), 0.0))

        strip(rows_of)

    def round_c():
        def rows_of(at, start):
            t_ref[at, :] = m_ref[at, :] - dot3(split(g_ref[at, :]), (m_hi[...], m_lo[...]), NN)

        strip(rows_of)
        strip(lambda at, start: keep_m(at, t_ref[at, :]))

    def weigh():
        inverse = (m_hi[...], m_lo[...])
        row, col = places(me * rows, (rows, lead))
        value = dot3(split(xbuf[me]), inverse, NT)
        value = jnp.where(col <= row, value, 0.0)
        out_ref[0, :, :lead] = value
        value = jnp.where(col < row // tile * tile, value, 0.0)
        w_hi[...], w_lo[...] = split(dot3(split(value), inverse, NN))

    def rest_panels():
        for zz in range(8, NZ):
            x_pass_up(zz).wait_recv()
            x_pass_down(zz).wait_recv()

    def subtract(g):
        weights = (w_hi[...], w_lo[...])

        def one(n, carry):
            cell = g * WIDE + n
            block = xbuf[pl.ds(lead // rows + tile // rows * cell, tile // rows)].reshape(tile, lead)
            at = pl.ds(pl.multiple_of(lead + cell * tile, tile), tile)
            out_ref[0, :, at] = front_ref[0, :, at] - dot3(weights, split(block), NT)
            return carry

        lax.fori_loop(0, WIDE, one, 0)

    todo = [load_lead, begin]
    for _ in range(ROUNDS - 1):
        todo += [round_a, round_b, round_c]
    todo += [weigh, rest_panels] + [lambda g=g: subtract(g) for g in range(CHUNKS)]

    def work(count):
        for _ in range(count):
            if todo:
                todo.pop(0)()

    def raw_start(way, j, own):
        copies = raw_go(way, j)
        count = len(copies) if j == 0 else 2
        for copy in copies[:count] if own else copies[count:]:
            copy.start()

    def raw_recv(j):
        for way in range(2):
            for copy in raw_go(way, j):
                copy.wait_recv()

    def raw_own(j):
        for way in range(2):
            wait_y(far_of(way, j))
            raw_start(way, j, True)

    def raw_forward(j):
        raw_recv(j - 1)
        for way in range(2):
            raw_start(way, j, False)

    for far in (8, 7, 9, 6, 10, 5, 11):
        pack(far)
    x_step(1)
    wait_y(8)
    for way in range(2):
        raw_start(way, 0, True)
    for far in (4, 12, 3, 13, 2, 14, 1, 15, 0):
        pack(far)
    x_step(2)
    raw_own(1)
    x_step(3)
    raw_forward(1)
    x_step(4)
    raw_own(2)
    x_step(5)
    raw_forward(2)
    x_step(6)
    raw_recv(2)
    for way in range(2):
        wait_y(far_of(way, 3))
    items = [own_items(far_of(way, 3)) + raw_items(way, far_of(way, 3)) for way in range(2)]
    for g in range(CHUNKS):
        for way in range(2):
            merge(dense.at[way, 0], True, items[way], g)
            go(way, 3, g).start()
        if g == 1:
            x_step(7)
    x_step(8)
    for zz in range(8):
        x_out(zz)
    outs, passes = list(range(8, NZ)), list(range(NZ))
    for j in range(4, 8):
        for way in range(2):
            wait_y(far_of(way, j))
        items = [own_items(far_of(way, j)) for way in range(2)]
        for g in range(CHUNKS):
            for way in range(2):
                go(way, j - 1, g).wait_recv()
                merge(dense.at[way, j - 3], False, items[way], g)
                go(way, j, g).start()
            slot_at = (j - 4) * CHUNKS + g
            if slot_at > 0:
                for zz in passes[:2]:
                    x_pass(zz)
                del passes[:2]
                for zz in outs[:2]:
                    x_out(zz)
                del outs[:2]
            if slot_at > 5:
                work(3)

    while todo:
        work(1)
    wait_y(0)
    items = own_items(0)
    for g in range(CHUNKS):
        for way in range(2):
            go(way, 7, g).wait_recv()

        def last(n, carry):
            cell = g * WIDE + n
            at = pl.ds(pl.multiple_of(lead + cell * tile, tile), tile)
            total = add(dense[0, 5, cell] + dense[1, 5, cell], items, cell)
            out_ref[0, :, at] = out_ref[0, :, at] + total
            return carry

        lax.fori_loop(0, WIDE, last, 0)

    for zz in range(NZ):
        for copy in (x_up(zz), x_down(zz), x_pass_up(zz), x_pass_down(zz)):
            copy.wait_send()
        for dy in range(1, NY):
            over_y(zz, dy).wait_send()
    for s in range(8):
        x_right(s).wait_send()
        if s < 7:
            x_left(s).wait_send()
    for way in range(2):
        for j in range(3):
            for copy in raw_go(way, j):
                copy.wait_send()
        for j in range(3, 8):
            for g in range(CHUNKS):
                go(way, j, g).wait_send()


def exchange(front, own_tiles, partner_tiles, pick, cols, lead):
    rows = front.shape[1]
    tile = own_tiles.shape[-1]
    slots = own_tiles.shape[1]
    sem = pltpu.SemaphoreType.DMA
    any_spec = pl.BlockSpec(memory_space=pl.ANY)
    smem = pl.BlockSpec(memory_space=pltpu.SMEM)
    vmem = pl.BlockSpec(memory_space=pltpu.VMEM)
    f32, bf16 = jnp.float32, jnp.bfloat16
    return pl.pallas_call(
        exchange_kernel,
        out_shape=jax.ShapeDtypeStruct(front.shape, f32),
        in_specs=[vmem, any_spec, any_spec, smem, smem],
        out_specs=vmem,
        scratch_shapes=[
            pltpu.VMEM((2 * slots + 1, tile, tile), f32),
            pltpu.VMEM((NZ, NY, 2, rows, tile), f32),
            pltpu.VMEM((NZ, 2 * NY - 2, rows, tile), f32),
            pltpu.VMEM((2, 4, rows, tile), f32),
            pltpu.VMEM((2, 12, rows, tile), f32),
            pltpu.VMEM((2, 20, rows, tile), f32),
            pltpu.VMEM((2, 6, CELLS, rows, tile), f32),
            pltpu.VMEM((NY * NZ, rows, lead), f32),
        ]
        + [pltpu.VMEM((lead, lead), f32)] * 4
        + [pltpu.VMEM((lead, lead), bf16)] * 4
        + [pltpu.VMEM((rows, lead), bf16)] * 2
        + [
            sem, sem, sem,
            sem((NZ, NY - 1)), sem((NZ, NY - 1)),
            sem((2, 3, 3)), sem((2, 3, 3)),
            sem((2, 5, CHUNKS)), sem((2, 5, CHUNKS)),
            sem((8,)), sem((8,)), sem((7,)), sem((7,)),
        ] + [sem((NZ,))] * 8,
        compiler_params=pltpu.CompilerParams(
            collective_id=0, has_side_effects=True, vmem_limit_bytes=56 * 2**20
        ),
    )(front, own_tiles, partner_tiles, pick, cols)


def body(front, own_tiles, partner_tiles, tile_rows, tile_cols, live):
    position = lax.axis_index("cube")
    front_pos = lax.axis_index("front")
    tile = own_tiles.shape[-1]
    slots = own_tiles.shape[1]
    tile_count = front.shape[2] // tile
    y, z = position // NZ, position % NZ

    rows_here = lax.dynamic_index_in_dim(tile_rows, front_pos, 0, keepdims=False)[:, :, 0]
    cols_here = lax.dynamic_index_in_dim(tile_cols, front_pos, 0, keepdims=False)
    live_here = lax.dynamic_index_in_dim(live, front_pos, 0, keepdims=False)
    within = jnp.arange(slots)
    rows_here = rows_here.reshape(NY * NZ, 2, slots)
    cols_here = cols_here.reshape(NY * NZ, 2, slots)
    rows_here = jnp.where(within < live_here[:, :, None], rows_here, -1)
    rows_mine = lax.dynamic_index_in_dim(rows_here, position, 0, keepdims=False)
    hit = rows_mine[:, :, None] == jnp.arange(tile_count)
    spot = within[None, :] + slots * jnp.arange(2)[:, None] - 2 * slots
    pick = jnp.sum(jnp.where(hit, spot[:, :, None], 0), axis=1) + 2 * slots
    hit = rows_here[None] == (y * (NZ // 2) + jnp.arange(NZ // 2))[:, None, None, None]
    cols = jnp.sum(jnp.where(hit, cols_here - (PANELS - 1), 0), axis=3) - 1
    cols = cols.reshape(NZ // 2, NY, NZ, 2).transpose(2, 0, 1, 3).reshape(NZ * NZ // 2, 2 * NY)
    return exchange(front, own_tiles, partner_tiles, pick, cols, PANELS * tile)


def solution(mesh):
    in_specs = (
        P("front", "cube", None),
        P("front", "cube", None, None),
        P("front", "cube", None, None),
        P(),
        P(),
        P(),
    )
    out_specs = P("front", "cube", None)
    return jax.shard_map(body, mesh=mesh, in_specs=in_specs, out_specs=out_specs, check_vma=False)
```

```python
import jax
import jax.numpy as jnp
from jax import lax
from jax.experimental import pallas as pl
from jax.experimental.pallas import tpu as pltpu
from jax.sharding import PartitionSpec as P

PANELS = 4
NY = 4
NZ = 16
CELLS = 28
CHUNKS = 4
WIDE = CELLS // CHUNKS
ROUNDS = 6
COARSE = 2
SUB = 128
MESH = pl.DeviceIdType.MESH
NN = (((1,), (0,)), ((), ()))
NT = (((1,), (1,)), ((), ()))


def split(value):
    high = value.astype(jnp.bfloat16)
    return high, (value - high.astype(jnp.float32)).astype(jnp.bfloat16)


def dot1(left, right, dims):
    return lax.dot_general(left, right, dims, preferred_element_type=jnp.float32)


def dot3(left, right, dims):
    small = dot1(left[0], right[1], dims) + dot1(left[1], right[0], dims)
    return small + dot1(left[0], right[0], dims)


def exchange_kernel(
    front_ref, own_ref, partner_ref, pick_ref, cols_ref, out_ref,
    tiles, packed, ybuf, raw1, raw2, raw3, dense, xbuf,
    lead_ref, m_ref, t_ref, g_ref, a_hi, a_lo, m_hi, m_lo, w_hi, w_lo,
    load_sem, pair_s, pair_r, y_s, y_r, raw_s, raw_r, d_s, d_r,
    zr_s, zr_r, zl_s, zl_r, yp_s, yp_r, ym_s, ym_r, fp_s, fp_r, fm_s, fm_r,
):
    me = lax.axis_index("cube")
    side = lax.axis_index("front")
    y, z = me // NZ, me % NZ
    rows, lead = xbuf.shape[1], xbuf.shape[2]
    slots = own_ref.shape[1]
    none = 2 * slots
    tile = tiles.shape[1]

    def dev(dy, dz):
        return {"cube": (y + dy) % NY * NZ + (z + dz) % NZ}

    mate = {"front": side + 1 - 2 * (side % 2)}
    toward = [dev(0, 1), dev(0, NZ - 1)]
    peers = toward + [dev(1, 0), dev(2, 0), dev(3, 0), mate]
    barrier = pltpu.get_barrier_semaphore()
    for peer in peers:
        pl.semaphore_signal(barrier, inc=1, device_id=peer, device_id_type=MESH)
    xbuf[me] = front_ref[0, :, :lead]
    pl.semaphore_wait(barrier, len(peers))

    def remote(src, dst, send, recv, to):
        return pltpu.make_async_remote_copy(
            src_ref=src, dst_ref=dst, send_sem=send, recv_sem=recv, device_id=to, device_id_type=MESH
        )

    pair = remote(partner_ref.at[0], tiles.at[pl.ds(slots, slots)], pair_s, pair_r, mate)
    pair.start()
    own = pltpu.make_async_copy(own_ref.at[0], tiles.at[pl.ds(0, slots)], load_sem)
    own.start()

    def slot(dy, zz):
        return xbuf.at[(y + dy) % NY * NZ + zz]

    def x_right(s):
        ref = slot(0, (z + NZ - s) % NZ)
        return remote(ref, ref, zr_s.at[s], zr_r.at[s], toward[0])

    def x_left(s):
        ref = slot(0, (z + s) % NZ)
        return remote(ref, ref, zl_s.at[s], zl_r.at[s], toward[1])

    def x_up(zz):
        ref = slot(0, zz)
        return remote(ref, ref, yp_s.at[zz], yp_r.at[zz], dev(1, 0))

    def x_down(zz):
        ref = slot(0, zz)
        return remote(ref, ref, ym_s.at[zz], ym_r.at[zz], dev(3, 0))

    def x_pass_up(zz):
        ref = slot(3, zz).at[pl.ds(0, rows // 2)]
        return remote(ref, ref, fp_s.at[zz], fp_r.at[zz], dev(1, 0))

    def x_pass_down(zz):
        ref = slot(1, zz).at[pl.ds(rows // 2, rows // 2)]
        return remote(ref, ref, fm_s.at[zz], fm_r.at[zz], dev(3, 0))

    def x_out(zz):
        x_up(zz).start()
        x_down(zz).start()

    def x_pass(zz):
        x_up(zz).wait_recv()
        x_pass_up(zz).start()
        x_down(zz).wait_recv()
        x_pass_down(zz).start()

    def x_step(s):
        x_right(s - 1).wait_recv()
        if s < 8:
            x_right(s).start()
            x_left(s - 1).wait_recv()
            if s < 7:
                x_left(s).start()

    x_right(0).start()
    x_left(0).start()
    tiles[none] = jnp.zeros(tiles.shape[1:], jnp.float32)
    own.wait()
    pair.wait()

    def over_y(far, dy):
        return remote(
            packed.at[far, (y + dy) % NY], ybuf.at[far, pl.ds(2 * dy - 2, 2)],
            y_s.at[far, dy - 1], y_r.at[far, dy - 1], dev(dy, 0),
        )

    def pack(far):
        there = (z + far) % NZ
        top = pl.multiple_of(there % 2 * rows, rows)
        for to_y in range(NY):
            for child in range(2):
                index = pick_ref[child, to_y * (NZ // 2) + there // 2]
                packed[far, to_y, child] = tiles[index, pl.ds(top, rows), :]
        for dy in range(1, NY):
            over_y(far, dy).start()

    def wait_y(far):
        for dy in range(1, NY):
            over_y(far, dy).wait_recv()

    def far_of(way, j):
        return (8 - j if way == 0 else 8 + j) % NZ

    half_list = 4

    def raw_go(way, j):
        far = far_of(way, j)
        to = toward[way]
        dst = (raw1, raw2, raw3)[j]
        mine = packed.at[far, y]
        theirs = ybuf.at[far]
        if j == 0:
            if way == 0:
                pairs = [(mine, pl.ds(0, 2)), (theirs.at[pl.ds(0, 2)], pl.ds(2, 2))]
            else:
                pairs = [(theirs.at[pl.ds(2, 4)], pl.ds(0, 4))]
        else:
            before = (raw1, raw2)[j - 1]
            count = before.shape[1]
            pairs = [(mine, pl.ds(0, 2)), (theirs, pl.ds(2, 6)), (before.at[way], pl.ds(8, count))]
        return [
            remote(a, dst.at[way, b], raw_s.at[way, j, n], raw_r.at[way, j, n], to)
            for n, (a, b) in enumerate(pairs)
        ]

    def cells(g):
        return pl.ds(g * WIDE, WIDE)

    def go(way, j, g):
        return remote(
            dense.at[way, j - 3, cells(g)], dense.at[way, j - 2, cells(g)],
            d_s.at[way, j - 3, g], d_r.at[way, j - 3, g], toward[way],
        )

    def list_cols(far_dest, dz, members):
        there = (z + far_dest) % NZ
        at = (z + dz) % NZ * (NZ // 2) + there // 2
        return [cols_ref[at, (y + NY - dy) % NY * 2 + child] for dy, child in members]

    full = [(dy, child) for dy in range(NY) for child in range(2)]

    def own_items(far):
        cols = list_cols(far, 0, full)
        refs = [packed.at[far, y, c] if dy == 0 else ybuf.at[far, 2 * dy - 2 + c] for dy, c in full]
        return list(zip(cols, refs))

    def raw_items(way, far):
        step = NZ - 1 if way == 0 else 1
        last = full[:half_list] if way == 0 else full[half_list:]
        cols = list_cols(far, step, full) + list_cols(far, 2 * step, full) + list_cols(far, 3 * step, last)
        return [(col, raw3.at[way, n]) for n, col in enumerate(cols)]

    def add(total, items, cell):
        for col, ref in items:
            total = total + (col == cell).astype(jnp.float32) * ref[...]
        return total

    def merge(buf, fresh, items, g):
        def one(n, carry):
            cell = g * WIDE + n
            start = jnp.zeros(buf.shape[1:], jnp.float32) if fresh else buf[cell]
            buf[cell] = add(start, items, cell)
            return carry

        lax.fori_loop(0, WIDE, one, 0)

    def strip(body):
        def one(n, carry):
            body(pl.ds(pl.multiple_of(n * SUB, SUB), SUB), n * SUB)
            return carry

        lax.fori_loop(0, lead // SUB, one, 0)

    def places(start, shape):
        row = lax.broadcasted_iota(jnp.int32, shape, 0) + start
        col = lax.broadcasted_iota(jnp.int32, shape, 1)
        return row, col

    def load_lead():
        for zz in range(8):
            x_pass_up(zz).wait_recv()
            x_pass_down(zz).wait_recv()

        def rows_of(at, start):
            block = xbuf[pl.ds(start // rows, SUB // rows)].reshape(SUB, lead)
            lead_ref[at, :] = block
            a_hi[at, :], a_lo[at, :] = split(block)

        strip(rows_of)

    def keep_m(at, value):
        m_ref[at, :] = value
        m_hi[at, :], m_lo[at, :] = split(value)

    def begin():
        def diagonal(at, start):
            row, col = places(start, (SUB, lead))
            t_ref[at, :] = jnp.where(row == col, lead_ref[at, :], 0.0)

        strip(diagonal)
        across = lax.rsqrt(jnp.sum(t_ref[...], axis=0, keepdims=True))

        def rows_of(at, start):
            row, col = places(start, (SUB, lead))
            down = lax.rsqrt(jnp.sum(t_ref[at, :], axis=1, keepdims=True))
            lower = jnp.where(row > col, lead_ref[at, :] * down, 0.0)
            unit = (row == col).astype(jnp.float32)
            diag = jnp.where(row == col, lead_ref[at, :], 0.0) * down * across
            keep_m(at, (unit - lower * across - 0.5 * (diag - unit)) * across)

        strip(rows_of)

    def round_of(exact):
        def pair(high, low):
            return (high, low) if exact else (high,)

        def product(left, right, dims):
            return dot3(left, right, dims) if exact else dot1(left[0], right[0], dims)

        def each(body):
            for n in range(lead // SUB):
                body(pl.ds(n * SUB, SUB), pl.ds(0, (n + 1) * SUB), n * SUB)

        def round_a():
            def rows_of(at, upto, start):
                left = pair(m_hi[at, upto], m_lo[at, upto])
                t_ref[at, upto] = product(left, pair(a_hi[upto, upto], a_lo[upto, upto]), NN)

            each(rows_of)

        def round_b():
            def rows_of(at, upto, start):
                gap = product(split(t_ref[at, upto]), pair(m_hi[upto, upto], m_lo[upto, upto]), NT)
                row, col = places(start, gap.shape)
                g_ref[at, upto] = jnp.where(row > col, gap, jnp.where(row == col, 0.5 * (gap - 1.0), 0.0))

            each(rows_of)

        def round_c():
            def rows_of(at, upto, start):
                fix = product(split(g_ref[at, upto]), pair(m_hi[upto, upto], m_lo[upto, upto]), NN)
                t_ref[at, upto] = m_ref[at, upto] - fix

            each(rows_of)

            def keep(at, upto, start):
                value = t_ref[at, upto]
                m_ref[at, upto] = value
                m_hi[at, upto], m_lo[at, upto] = split(value)

            each(keep)

        return [round_a, round_b, round_c]

    def weigh():
        inverse = (m_hi[...], m_lo[...])
        row, col = places(me * rows, (rows, lead))
        value = dot3(split(xbuf[me]), inverse, NT)
        value = jnp.where(col <= row, value, 0.0)
        out_ref[0, :, :lead] = value
        value = jnp.where(col < row // tile * tile, value, 0.0)
        w_hi[...], w_lo[...] = split(dot3(split(value), inverse, NN))

    def rest_panels():
        for zz in range(8, NZ):
            x_pass_up(zz).wait_recv()
            x_pass_down(zz).wait_recv()

    def subtract(g):
        weights = (w_hi[...], w_lo[...])

        def one(n, carry):
            cell = g * WIDE + n
            block = xbuf[pl.ds(lead // rows + tile // rows * cell, tile // rows)].reshape(tile, lead)
            at = pl.ds(pl.multiple_of(lead + cell * tile, tile), tile)
            out_ref[0, :, at] = front_ref[0, :, at] - dot3(weights, split(block), NT)
            return carry

        lax.fori_loop(0, WIDE, one, 0)

    todo = [load_lead, begin]
    for n in range(1, ROUNDS):
        todo += round_of(n > COARSE)
    todo += [weigh, rest_panels] + [lambda g=g: subtract(g) for g in range(CHUNKS)]

    def work(count):
        for _ in range(count):
            if todo:
                todo.pop(0)()

    def raw_start(way, j, own):
        copies = raw_go(way, j)
        count = len(copies) if j == 0 else 2
        for copy in copies[:count] if own else copies[count:]:
            copy.start()

    def raw_recv(j):
        for way in range(2):
            for copy in raw_go(way, j):
                copy.wait_recv()

    def raw_own(j):
        for way in range(2):
            wait_y(far_of(way, j))
            raw_start(way, j, True)

    def raw_forward(j):
        raw_recv(j - 1)
        for way in range(2):
            raw_start(way, j, False)

    for far in (8, 7, 9, 6, 10, 5, 11):
        pack(far)
    x_step(1)
    wait_y(8)
    for way in range(2):
        raw_start(way, 0, True)
    for far in (4, 12, 3, 13, 2, 14, 1, 15, 0):
        pack(far)
    x_step(2)
    raw_own(1)
    x_step(3)
    raw_forward(1)
    x_step(4)
    raw_own(2)
    x_step(5)
    raw_forward(2)
    x_step(6)
    raw_recv(2)
    for way in range(2):
        wait_y(far_of(way, 3))
    items = [own_items(far_of(way, 3)) + raw_items(way, far_of(way, 3)) for way in range(2)]
    for g in range(CHUNKS):
        for way in range(2):
            merge(dense.at[way, 0], True, items[way], g)
            go(way, 3, g).start()
        if g == 1:
            x_step(7)
    x_step(8)
    for zz in range(8):
        x_out(zz)
    outs, passes = list(range(8, NZ)), list(range(NZ))
    for j in range(4, 8):
        for way in range(2):
            wait_y(far_of(way, j))
        items = [own_items(far_of(way, j)) for way in range(2)]
        for g in range(CHUNKS):
            for way in range(2):
                go(way, j - 1, g).wait_recv()
                merge(dense.at[way, j - 3], False, items[way], g)
                go(way, j, g).start()
            slot_at = (j - 4) * CHUNKS + g
            if slot_at > 0:
                for zz in passes[:2]:
                    x_pass(zz)
                del passes[:2]
                for zz in outs[:2]:
                    x_out(zz)
                del outs[:2]
            if slot_at > 5:
                work(2 if slot_at < 12 else 3)

    while todo:
        work(1)
    wait_y(0)
    items = own_items(0)
    for g in range(CHUNKS):
        for way in range(2):
            go(way, 7, g).wait_recv()

        def last(n, carry):
            cell = g * WIDE + n
            at = pl.ds(pl.multiple_of(lead + cell * tile, tile), tile)
            total = add(dense[0, 5, cell] + dense[1, 5, cell], items, cell)
            out_ref[0, :, at] = out_ref[0, :, at] + total
            return carry

        lax.fori_loop(0, WIDE, last, 0)

    for zz in range(NZ):
        for copy in (x_up(zz), x_down(zz), x_pass_up(zz), x_pass_down(zz)):
            copy.wait_send()
        for dy in range(1, NY):
            over_y(zz, dy).wait_send()
    for s in range(8):
        x_right(s).wait_send()
        if s < 7:
            x_left(s).wait_send()
    for way in range(2):
        for j in range(3):
            for copy in raw_go(way, j):
                copy.wait_send()
        for j in range(3, 8):
            for g in range(CHUNKS):
                go(way, j, g).wait_send()


def exchange(front, own_tiles, partner_tiles, pick, cols, lead):
    rows = front.shape[1]
    tile = own_tiles.shape[-1]
    slots = own_tiles.shape[1]
    sem = pltpu.SemaphoreType.DMA
    any_spec = pl.BlockSpec(memory_space=pl.ANY)
    smem = pl.BlockSpec(memory_space=pltpu.SMEM)
    vmem = pl.BlockSpec(memory_space=pltpu.VMEM)
    f32, bf16 = jnp.float32, jnp.bfloat16
    return pl.pallas_call(
        exchange_kernel,
        out_shape=jax.ShapeDtypeStruct(front.shape, f32),
        in_specs=[vmem, any_spec, any_spec, smem, smem],
        out_specs=vmem,
        scratch_shapes=[
            pltpu.VMEM((2 * slots + 1, tile, tile), f32),
            pltpu.VMEM((NZ, NY, 2, rows, tile), f32),
            pltpu.VMEM((NZ, 2 * NY - 2, rows, tile), f32),
            pltpu.VMEM((2, 4, rows, tile), f32),
            pltpu.VMEM((2, 12, rows, tile), f32),
            pltpu.VMEM((2, 20, rows, tile), f32),
            pltpu.VMEM((2, 6, CELLS, rows, tile), f32),
            pltpu.VMEM((NY * NZ, rows, lead), f32),
        ]
        + [pltpu.VMEM((lead, lead), f32)] * 4
        + [pltpu.VMEM((lead, lead), bf16)] * 4
        + [pltpu.VMEM((rows, lead), bf16)] * 2
        + [
            sem, sem, sem,
            sem((NZ, NY - 1)), sem((NZ, NY - 1)),
            sem((2, 3, 3)), sem((2, 3, 3)),
            sem((2, 5, CHUNKS)), sem((2, 5, CHUNKS)),
            sem((8,)), sem((8,)), sem((7,)), sem((7,)),
        ] + [sem((NZ,))] * 8,
        compiler_params=pltpu.CompilerParams(
            collective_id=0, has_side_effects=True, vmem_limit_bytes=56 * 2**20
        ),
    )(front, own_tiles, partner_tiles, pick, cols)


def body(front, own_tiles, partner_tiles, tile_rows, tile_cols, live):
    position = lax.axis_index("cube")
    front_pos = lax.axis_index("front")
    tile = own_tiles.shape[-1]
    slots = own_tiles.shape[1]
    tile_count = front.shape[2] // tile
    y, z = position // NZ, position % NZ

    rows_here = lax.dynamic_index_in_dim(tile_rows, front_pos, 0, keepdims=False)[:, :, 0]
    cols_here = lax.dynamic_index_in_dim(tile_cols, front_pos, 0, keepdims=False)
    live_here = lax.dynamic_index_in_dim(live, front_pos, 0, keepdims=False)
    within = jnp.arange(slots)
    rows_here = rows_here.reshape(NY * NZ, 2, slots)
    cols_here = cols_here.reshape(NY * NZ, 2, slots)
    rows_here = jnp.where(within < live_here[:, :, None], rows_here, -1)
    rows_mine = lax.dynamic_index_in_dim(rows_here, position, 0, keepdims=False)
    hit = rows_mine[:, :, None] == jnp.arange(tile_count)
    spot = within[None, :] + slots * jnp.arange(2)[:, None] - 2 * slots
    pick = jnp.sum(jnp.where(hit, spot[:, :, None], 0), axis=1) + 2 * slots
    hit = rows_here[None] == (y * (NZ // 2) + jnp.arange(NZ // 2))[:, None, None, None]
    cols = jnp.sum(jnp.where(hit, cols_here - (PANELS - 1), 0), axis=3) - 1
    cols = cols.reshape(NZ // 2, NY, NZ, 2).transpose(2, 0, 1, 3).reshape(NZ * NZ // 2, 2 * NY)
    return exchange(front, own_tiles, partner_tiles, pick, cols, PANELS * tile)


def solution(mesh):
    in_specs = (
        P("front", "cube", None),
        P("front", "cube", None, None),
        P("front", "cube", None, None),
        P(),
        P(),
        P(),
    )
    out_specs = P("front", "cube", None)
    return jax.shard_map(body, mesh=mesh, in_specs=in_specs, out_specs=out_specs, check_vma=False)
```

```python
import jax
import jax.numpy as jnp
from jax import lax
from jax.experimental import pallas as pl
from jax.experimental.pallas import tpu as pltpu
from jax.sharding import PartitionSpec as P

PANELS = 4
NY = 4
NZ = 16
CELLS = 28
CHUNKS = 4
WIDE = CELLS // CHUNKS
ROUNDS = 6
COARSE = 2
SUB = 128
MESH = pl.DeviceIdType.MESH
NN = (((1,), (0,)), ((), ()))
NT = (((1,), (1,)), ((), ()))


def split(value):
    high = value.astype(jnp.bfloat16)
    return high, (value - high.astype(jnp.float32)).astype(jnp.bfloat16)


def dot1(left, right, dims):
    return lax.dot_general(left, right, dims, preferred_element_type=jnp.float32)


def dot3(left, right, dims):
    small = dot1(left[0], right[1], dims) + dot1(left[1], right[0], dims)
    return small + dot1(left[0], right[0], dims)


def exchange_kernel(
    front_ref, own_ref, partner_ref, pick_ref, cols_ref, out_ref,
    tiles, packed, ybuf, raw1, raw2, raw3, dense, xbuf,
    lead_ref, m_ref, t_ref, g_ref, a_hi, a_lo, m_hi, m_lo, w_hi, w_lo,
    load_sem, pair_s, pair_r, y_s, y_r, raw_s, raw_r, d_s, d_r,
    zr_s, zr_r, zl_s, zl_r, yp_s, yp_r, ym_s, ym_r, fp_s, fp_r, fm_s, fm_r,
):
    me = lax.axis_index("cube")
    side = lax.axis_index("front")
    y, z = me // NZ, me % NZ
    rows, lead = xbuf.shape[1], xbuf.shape[2]
    slots = own_ref.shape[1]
    none = 2 * slots
    tile = tiles.shape[1]

    def dev(dy, dz):
        return {"cube": (y + dy) % NY * NZ + (z + dz) % NZ}

    mate = {"front": side + 1 - 2 * (side % 2)}
    toward = [dev(0, 1), dev(0, NZ - 1)]
    peers = toward + [dev(1, 0), dev(2, 0), dev(3, 0), mate]
    barrier = pltpu.get_barrier_semaphore()
    for peer in peers:
        pl.semaphore_signal(barrier, inc=1, device_id=peer, device_id_type=MESH)
    mine = pltpu.make_async_copy(front_ref.at[0, :, pl.ds(0, lead)], xbuf.at[me], load_sem.at[1])
    mine.start()
    own = pltpu.make_async_copy(own_ref.at[0], tiles.at[pl.ds(0, slots)], load_sem.at[0])
    own.start()
    pl.semaphore_wait(barrier, len(peers))

    def remote(src, dst, send, recv, to):
        return pltpu.make_async_remote_copy(
            src_ref=src, dst_ref=dst, send_sem=send, recv_sem=recv, device_id=to, device_id_type=MESH
        )

    pair = remote(partner_ref.at[0], tiles.at[pl.ds(slots, slots)], pair_s, pair_r, mate)
    pair.start()
    mine.wait()

    def slot(dy, zz):
        return xbuf.at[(y + dy) % NY * NZ + zz]

    def x_right(s):
        ref = slot(0, (z + NZ - s) % NZ)
        return remote(ref, ref, zr_s.at[s], zr_r.at[s], toward[0])

    def x_left(s):
        ref = slot(0, (z + s) % NZ)
        return remote(ref, ref, zl_s.at[s], zl_r.at[s], toward[1])

    def x_up(zz):
        ref = slot(0, zz)
        return remote(ref, ref, yp_s.at[zz], yp_r.at[zz], dev(1, 0))

    def x_down(zz):
        ref = slot(0, zz)
        return remote(ref, ref, ym_s.at[zz], ym_r.at[zz], dev(3, 0))

    def x_pass_up(zz):
        ref = slot(3, zz).at[pl.ds(0, rows // 2)]
        return remote(ref, ref, fp_s.at[zz], fp_r.at[zz], dev(1, 0))

    def x_pass_down(zz):
        ref = slot(1, zz).at[pl.ds(rows // 2, rows // 2)]
        return remote(ref, ref, fm_s.at[zz], fm_r.at[zz], dev(3, 0))

    def x_out(zz):
        x_up(zz).start()
        x_down(zz).start()

    def x_pass(zz):
        x_up(zz).wait_recv()
        x_pass_up(zz).start()
        x_down(zz).wait_recv()
        x_pass_down(zz).start()

    def x_step(s):
        x_right(s - 1).wait_recv()
        if s < 8:
            x_right(s).start()
            x_left(s - 1).wait_recv()
            if s < 7:
                x_left(s).start()

    x_right(0).start()
    x_left(0).start()
    tiles[none] = jnp.zeros(tiles.shape[1:], jnp.float32)
    own.wait()
    pair.wait()

    def over_y(far, dy):
        return remote(
            packed.at[far, (y + dy) % NY], ybuf.at[far, pl.ds(2 * dy - 2, 2)],
            y_s.at[far, dy - 1], y_r.at[far, dy - 1], dev(dy, 0),
        )

    def pack(far):
        there = (z + far) % NZ
        top = pl.multiple_of(there % 2 * rows, rows)
        for to_y in range(NY):
            for child in range(2):
                index = pick_ref[child, to_y * (NZ // 2) + there // 2]
                packed[far, to_y, child] = tiles[index, pl.ds(top, rows), :]
        for dy in range(1, NY):
            over_y(far, dy).start()

    def wait_y(far):
        for dy in range(1, NY):
            over_y(far, dy).wait_recv()

    def far_of(way, j):
        return (8 - j if way == 0 else 8 + j) % NZ

    half_list = 4

    def raw_go(way, j):
        far = far_of(way, j)
        to = toward[way]
        dst = (raw1, raw2, raw3)[j]
        mine = packed.at[far, y]
        theirs = ybuf.at[far]
        if j == 0:
            if way == 0:
                pairs = [(mine, pl.ds(0, 2)), (theirs.at[pl.ds(0, 2)], pl.ds(2, 2))]
            else:
                pairs = [(theirs.at[pl.ds(2, 4)], pl.ds(0, 4))]
        else:
            before = (raw1, raw2)[j - 1]
            count = before.shape[1]
            pairs = [(mine, pl.ds(0, 2)), (theirs, pl.ds(2, 6)), (before.at[way], pl.ds(8, count))]
        return [
            remote(a, dst.at[way, b], raw_s.at[way, j, n], raw_r.at[way, j, n], to)
            for n, (a, b) in enumerate(pairs)
        ]

    def cells(g):
        return pl.ds(g * WIDE, WIDE)

    def go(way, j, g):
        return remote(
            dense.at[way, j - 3, cells(g)], dense.at[way, j - 2, cells(g)],
            d_s.at[way, j - 3, g], d_r.at[way, j - 3, g], toward[way],
        )

    def list_cols(far_dest, dz, members):
        there = (z + far_dest) % NZ
        at = (z + dz) % NZ
        return [cols_ref[there // 2, (child * NY + (y + NY - dy) % NY) * NZ + at] for dy, child in members]

    full = [(dy, child) for dy in range(NY) for child in range(2)]

    def own_items(far):
        cols = list_cols(far, 0, full)
        refs = [packed.at[far, y, c] if dy == 0 else ybuf.at[far, 2 * dy - 2 + c] for dy, c in full]
        return list(zip(cols, refs))

    def raw_items(way, far):
        step = NZ - 1 if way == 0 else 1
        last = full[:half_list] if way == 0 else full[half_list:]
        cols = list_cols(far, step, full) + list_cols(far, 2 * step, full) + list_cols(far, 3 * step, last)
        return [(col, raw3.at[way, n]) for n, col in enumerate(cols)]

    def add(total, items, cell):
        for col, ref in items:
            total = total + (col == cell).astype(jnp.float32) * ref[...]
        return total

    def merge(buf, fresh, items, g):
        def one(n, carry):
            cell = g * WIDE + n
            start = jnp.zeros(buf.shape[1:], jnp.float32) if fresh else buf[cell]
            buf[cell] = add(start, items, cell)
            return carry

        lax.fori_loop(0, WIDE, one, 0)

    def strip(body):
        def one(n, carry):
            body(pl.ds(pl.multiple_of(n * SUB, SUB), SUB), n * SUB)
            return carry

        lax.fori_loop(0, lead // SUB, one, 0)

    def places(start, shape):
        row = lax.broadcasted_iota(jnp.int32, shape, 0) + start
        col = lax.broadcasted_iota(jnp.int32, shape, 1)
        return row, col

    def load_lead():
        for zz in range(8):
            x_pass_up(zz).wait_recv()
            x_pass_down(zz).wait_recv()

        def rows_of(at, start):
            block = xbuf[pl.ds(start // rows, SUB // rows)].reshape(SUB, lead)
            lead_ref[at, :] = block
            a_hi[at, :], a_lo[at, :] = split(block)

        strip(rows_of)

    def keep_m(at, value):
        m_ref[at, :] = value
        m_hi[at, :], m_lo[at, :] = split(value)

    def begin():
        def diagonal(at, start):
            row, col = places(start, (SUB, lead))
            t_ref[at, :] = jnp.where(row == col, lead_ref[at, :], 0.0)

        strip(diagonal)
        across = lax.rsqrt(jnp.sum(t_ref[...], axis=0, keepdims=True))

        def rows_of(at, start):
            row, col = places(start, (SUB, lead))
            down = lax.rsqrt(jnp.sum(t_ref[at, :], axis=1, keepdims=True))
            lower = jnp.where(row > col, lead_ref[at, :] * down, 0.0)
            unit = (row == col).astype(jnp.float32)
            diag = jnp.where(row == col, lead_ref[at, :], 0.0) * down * across
            keep_m(at, (unit - lower * across - 0.5 * (diag - unit)) * across)

        strip(rows_of)

    def round_of(exact):
        def pair(high, low):
            return (high, low) if exact else (high,)

        def product(left, right, dims):
            return dot3(left, right, dims) if exact else dot1(left[0], right[0], dims)

        def each(body):
            for n in range(lead // SUB):
                body(pl.ds(n * SUB, SUB), pl.ds(0, (n + 1) * SUB), n * SUB)

        def round_a():
            def rows_of(at, upto, start):
                left = pair(m_hi[at, upto], m_lo[at, upto])
                t_ref[at, upto] = product(left, pair(a_hi[upto, upto], a_lo[upto, upto]), NN)

            each(rows_of)

        def round_b():
            def rows_of(at, upto, start):
                gap = product(split(t_ref[at, upto]), pair(m_hi[upto, upto], m_lo[upto, upto]), NT)
                row, col = places(start, gap.shape)
                g_ref[at, upto] = jnp.where(row > col, gap, jnp.where(row == col, 0.5 * (gap - 1.0), 0.0))

            each(rows_of)

        def round_c():
            def rows_of(at, upto, start):
                fix = product(split(g_ref[at, upto]), pair(m_hi[upto, upto], m_lo[upto, upto]), NN)
                t_ref[at, upto] = m_ref[at, upto] - fix

            each(rows_of)

            def keep(at, upto, start):
                value = t_ref[at, upto]
                m_ref[at, upto] = value
                m_hi[at, upto], m_lo[at, upto] = split(value)

            each(keep)

        return [round_a, round_b, round_c]

    def weigh():
        inverse = (m_hi[...], m_lo[...])
        row, col = places(me * rows, (rows, lead))
        value = dot3(split(xbuf[me]), inverse, NT)
        value = jnp.where(col <= row, value, 0.0)
        out_ref[0, :, :lead] = value
        value = jnp.where(col < row // tile * tile, value, 0.0)
        w_hi[...], w_lo[...] = split(dot3(split(value), inverse, NN))

    def rest_panels():
        for zz in range(8, NZ):
            x_pass_up(zz).wait_recv()
            x_pass_down(zz).wait_recv()

    def subtract(g):
        weights = (w_hi[...], w_lo[...])

        def one(n, carry):
            cell = g * WIDE + n
            block = xbuf[pl.ds(lead // rows + tile // rows * cell, tile // rows)].reshape(tile, lead)
            at = pl.ds(pl.multiple_of(lead + cell * tile, tile), tile)
            out_ref[0, :, at] = -dot3(weights, split(block), NT)
            return carry

        lax.fori_loop(0, WIDE, one, 0)

    todo = [load_lead, begin]
    for n in range(1, ROUNDS):
        todo += round_of(n > COARSE)
    todo += [weigh, rest_panels] + [lambda g=g: subtract(g) for g in range(CHUNKS)]

    def work(count):
        for _ in range(count):
            if todo:
                todo.pop(0)()

    def raw_start(way, j, own):
        copies = raw_go(way, j)
        count = len(copies) if j == 0 else 2
        for copy in copies[:count] if own else copies[count:]:
            copy.start()

    def raw_recv(j):
        for way in range(2):
            for copy in raw_go(way, j):
                copy.wait_recv()

    def raw_own(j):
        for way in range(2):
            wait_y(far_of(way, j))
            raw_start(way, j, True)

    def raw_forward(j):
        raw_recv(j - 1)
        for way in range(2):
            raw_start(way, j, False)

    def packs(*members):
        for far in members:
            pack(far)

    packs(8)
    x_step(1)
    packs(7, 9)
    wait_y(8)
    for way in range(2):
        raw_start(way, 0, True)
    packs(6, 10)
    x_step(2)
    raw_own(1)
    packs(5, 11)
    x_step(3)
    raw_forward(1)
    packs(4, 12)
    x_step(4)
    raw_own(2)
    packs(3, 13)
    x_step(5)
    raw_forward(2)
    packs(2, 14)
    x_step(6)
    packs(1, 15, 0)
    raw_recv(2)
    for way in range(2):
        wait_y(far_of(way, 3))
    items = [own_items(far_of(way, 3)) + raw_items(way, far_of(way, 3)) for way in range(2)]
    for g in range(CHUNKS):
        for way in range(2):
            merge(dense.at[way, 0], True, items[way], g)
            go(way, 3, g).start()
        if g == 1:
            x_step(7)
    x_step(8)
    for zz in range(8):
        x_out(zz)
    outs, passes = list(range(8, NZ)), list(range(NZ))
    for j in range(4, 8):
        for way in range(2):
            wait_y(far_of(way, j))
        items = [own_items(far_of(way, j)) for way in range(2)]
        for g in range(CHUNKS):
            for way in range(2):
                go(way, j - 1, g).wait_recv()
                merge(dense.at[way, j - 3], False, items[way], g)
                go(way, j, g).start()
            slot_at = (j - 4) * CHUNKS + g
            if slot_at > 0:
                for zz in passes[:2]:
                    x_pass(zz)
                del passes[:2]
                for zz in outs[:2]:
                    x_out(zz)
                del outs[:2]
            if slot_at > 5:
                work(2 if slot_at < 12 else 3)

    while todo:
        work(1)
    wait_y(0)
    items = own_items(0)
    for g in range(CHUNKS):
        for way in range(2):
            go(way, 7, g).wait_recv()

        def last(n, carry):
            cell = g * WIDE + n
            at = pl.ds(pl.multiple_of(lead + cell * tile, tile), tile)
            total = add(dense[0, 5, cell] + dense[1, 5, cell], items, cell)
            out_ref[0, :, at] = out_ref[0, :, at] + total
            return carry

        lax.fori_loop(0, WIDE, last, 0)

    for zz in range(NZ):
        for copy in (x_up(zz), x_down(zz), x_pass_up(zz), x_pass_down(zz)):
            copy.wait_send()
        for dy in range(1, NY):
            over_y(zz, dy).wait_send()
    for s in range(8):
        x_right(s).wait_send()
        if s < 7:
            x_left(s).wait_send()
    for way in range(2):
        for j in range(3):
            for copy in raw_go(way, j):
                copy.wait_send()
        for j in range(3, 8):
            for g in range(CHUNKS):
                go(way, j, g).wait_send()


def exchange(front, own_tiles, partner_tiles, pick, cols, lead):
    rows = front.shape[1]
    tile = own_tiles.shape[-1]
    slots = own_tiles.shape[1]
    sem = pltpu.SemaphoreType.DMA
    any_spec = pl.BlockSpec(memory_space=pl.ANY)
    smem = pl.BlockSpec(memory_space=pltpu.SMEM)
    vmem = pl.BlockSpec(memory_space=pltpu.VMEM)
    f32, bf16 = jnp.float32, jnp.bfloat16
    return pl.pallas_call(
        exchange_kernel,
        out_shape=jax.ShapeDtypeStruct(front.shape, f32),
        in_specs=[any_spec, any_spec, any_spec, smem, smem],
        out_specs=vmem,
        scratch_shapes=[
            pltpu.VMEM((2 * slots + 1, tile, tile), f32),
            pltpu.VMEM((NZ, NY, 2, rows, tile), f32),
            pltpu.VMEM((NZ, 2 * NY - 2, rows, tile), f32),
            pltpu.VMEM((2, 4, rows, tile), f32),
            pltpu.VMEM((2, 12, rows, tile), f32),
            pltpu.VMEM((2, 20, rows, tile), f32),
            pltpu.VMEM((2, 6, CELLS, rows, tile), f32),
            pltpu.VMEM((NY * NZ, rows, lead), f32),
        ]
        + [pltpu.VMEM((lead, lead), f32)] * 4
        + [pltpu.VMEM((lead, lead), bf16)] * 4
        + [pltpu.VMEM((rows, lead), bf16)] * 2
        + [
            sem((2,)), sem, sem,
            sem((NZ, NY - 1)), sem((NZ, NY - 1)),
            sem((2, 3, 3)), sem((2, 3, 3)),
            sem((2, 5, CHUNKS)), sem((2, 5, CHUNKS)),
            sem((8,)), sem((8,)), sem((7,)), sem((7,)),
        ] + [sem((NZ,))] * 8,
        compiler_params=pltpu.CompilerParams(
            collective_id=0, has_side_effects=True, vmem_limit_bytes=56 * 2**20
        ),
    )(front, own_tiles, partner_tiles, pick, cols)


def body(front, own_tiles, partner_tiles, tile_rows, tile_cols, live):
    position = lax.axis_index("cube")
    front_pos = lax.axis_index("front")
    tile = own_tiles.shape[-1]
    slots = own_tiles.shape[1]
    tile_count = front.shape[2] // tile
    y, z = position // NZ, position % NZ

    rows_here = lax.dynamic_index_in_dim(tile_rows, front_pos, 0, keepdims=False)[:, :, 0]
    cols_here = lax.dynamic_index_in_dim(tile_cols, front_pos, 0, keepdims=False)
    live_here = lax.dynamic_index_in_dim(live, front_pos, 0, keepdims=False)
    within = jnp.arange(slots)
    rows_here = rows_here.reshape(NY * NZ, 2, slots)
    cols_here = cols_here.reshape(NY * NZ, 2, slots)
    rows_here = jnp.where(within < live_here[:, :, None], rows_here, -1)
    rows_mine = lax.dynamic_index_in_dim(rows_here, position, 0, keepdims=False)
    hit = rows_mine[:, :, None] == jnp.arange(tile_count)
    spot = within[None, :] + slots * jnp.arange(2)[:, None] - 2 * slots
    pick = jnp.sum(jnp.where(hit, spot[:, :, None], 0), axis=1) + 2 * slots
    rows_here = rows_here.transpose(1, 0, 2)
    cols_here = cols_here.transpose(1, 0, 2)
    hit = rows_here[None] == (y * (NZ // 2) + jnp.arange(NZ // 2))[:, None, None, None]
    cols = jnp.sum(jnp.where(hit, cols_here - (PANELS - 1), 0), axis=3) - 1
    cols = cols.reshape(NZ // 2, 2 * NY * NZ)
    lead = PANELS * tile
    change = exchange(front, own_tiles, partner_tiles, pick, cols, lead)
    factored = lax.broadcasted_iota(jnp.int32, change.shape, 2) < lead
    return jnp.where(factored, change, change + front)


def solution(mesh):
    in_specs = (
        P("front", "cube", None),
        P("front", "cube", None, None),
        P("front", "cube", None, None),
        P(),
        P(),
        P(),
    )
    out_specs = P("front", "cube", None)
    return jax.shard_map(body, mesh=mesh, in_specs=in_specs, out_specs=out_specs, check_vma=False)
```

```python
import jax
import jax.numpy as jnp
from jax import lax
from jax.experimental import pallas as pl
from jax.experimental.pallas import tpu as pltpu
from jax.sharding import PartitionSpec as P

PANELS = 4
NY = 4
NZ = 16
CELLS = 28
CHUNKS = 4
WIDE = CELLS // CHUNKS
ROUNDS = 6
COARSE = 2
SUB = 128
MESH = pl.DeviceIdType.MESH
NN = (((1,), (0,)), ((), ()))
NT = (((1,), (1,)), ((), ()))


def split(value):
    high = value.astype(jnp.bfloat16)
    return high, (value - high.astype(jnp.float32)).astype(jnp.bfloat16)


def dot1(left, right, dims):
    return lax.dot_general(left, right, dims, preferred_element_type=jnp.float32)


def dot3(left, right, dims):
    small = dot1(left[0], right[1], dims) + dot1(left[1], right[0], dims)
    return small + dot1(left[0], right[0], dims)


def fill_table(table, rows_ref, cols_ref, live_ref, side, y, me, slots):
    devices = rows_ref.shape[2]
    table[...] = jnp.zeros(table.shape, jnp.int32)
    spot = lax.broadcasted_iota(jnp.int32, (slots, devices), 0)
    lane = lax.broadcasted_iota(jnp.int32, (slots, devices), 1)
    wide_spot = lax.broadcasted_iota(jnp.int32, (slots, 128), 0)
    wide_lane = lax.broadcasted_iota(jnp.int32, (slots, 128), 1)
    for child in range(2):
        at = pl.ds(child * slots, slots)
        alive = spot < live_ref[side, pl.ds(child, 1), :]
        rows = jnp.where(alive, rows_ref[side, at, :], -1)
        cells = cols_ref[side, at, :] - (PANELS - 1)
        for q in range(NZ // 2):
            hit = rows == y * (NZ // 2) + q
            found = jnp.sum(jnp.where(hit, cells, 0), axis=0, keepdims=True) - 1
            table[pl.ds(2 * q + child, 1), pl.ds(0, devices)] = found
        mine = jnp.sum(jnp.where(lane == me, rows, 0), axis=1, keepdims=True)
        slot = wide_spot + (child * slots - 2 * slots)
        found = jnp.sum(jnp.where(mine == wide_lane, slot, 0), axis=0, keepdims=True)
        table[pl.ds(NZ + child, 1), :] = found + 2 * slots


def exchange_kernel(
    front_ref, own_ref, partner_ref, rows_ref, cols_ref, live_ref, out_ref,
    tiles, packed, ybuf, raw1, raw2, raw3, dense, xbuf,
    table, plan, lead_ref, m_ref, t_ref, g_ref, a_hi, a_lo, m_hi, m_lo, w_hi, w_lo,
    load_sem, pair_s, pair_r, y_s, y_r, raw_s, raw_r, d_s, d_r,
    zr_s, zr_r, zl_s, zl_r, yp_s, yp_r, ym_s, ym_r, fp_s, fp_r, fm_s, fm_r,
):
    me = lax.axis_index("cube")
    side = lax.axis_index("front")
    y, z = me // NZ, me % NZ
    rows, lead = xbuf.shape[1], xbuf.shape[2]
    slots = own_ref.shape[1]
    none = 2 * slots
    tile = tiles.shape[1]

    def dev(dy, dz):
        return {"cube": (y + dy) % NY * NZ + (z + dz) % NZ}

    mate = {"front": side + 1 - 2 * (side % 2)}
    toward = [dev(0, 1), dev(0, NZ - 1)]
    peers = toward + [dev(1, 0), dev(2, 0), dev(3, 0), mate]
    barrier = pltpu.get_barrier_semaphore()
    for peer in peers:
        pl.semaphore_signal(barrier, inc=1, device_id=peer, device_id_type=MESH)
    mine = pltpu.make_async_copy(front_ref.at[0, :, pl.ds(0, lead)], xbuf.at[me], load_sem.at[1])
    mine.start()
    own = pltpu.make_async_copy(own_ref.at[0], tiles.at[pl.ds(0, slots)], load_sem.at[0])
    own.start()
    fill_table(table, rows_ref, cols_ref, live_ref, side, y, me, slots)
    planned = pltpu.make_async_copy(table, plan, load_sem.at[2])
    planned.start()
    pl.semaphore_wait(barrier, len(peers))

    def remote(src, dst, send, recv, to):
        return pltpu.make_async_remote_copy(
            src_ref=src, dst_ref=dst, send_sem=send, recv_sem=recv, device_id=to, device_id_type=MESH
        )

    pair = remote(partner_ref.at[0], tiles.at[pl.ds(slots, slots)], pair_s, pair_r, mate)
    pair.start()
    mine.wait()

    def slot(dy, zz):
        return xbuf.at[(y + dy) % NY * NZ + zz]

    def x_right(s):
        ref = slot(0, (z + NZ - s) % NZ)
        return remote(ref, ref, zr_s.at[s], zr_r.at[s], toward[0])

    def x_left(s):
        ref = slot(0, (z + s) % NZ)
        return remote(ref, ref, zl_s.at[s], zl_r.at[s], toward[1])

    def x_up(zz):
        ref = slot(0, zz)
        return remote(ref, ref, yp_s.at[zz], yp_r.at[zz], dev(1, 0))

    def x_down(zz):
        ref = slot(0, zz)
        return remote(ref, ref, ym_s.at[zz], ym_r.at[zz], dev(3, 0))

    def x_pass_up(zz):
        ref = slot(3, zz).at[pl.ds(0, rows // 2)]
        return remote(ref, ref, fp_s.at[zz], fp_r.at[zz], dev(1, 0))

    def x_pass_down(zz):
        ref = slot(1, zz).at[pl.ds(rows // 2, rows // 2)]
        return remote(ref, ref, fm_s.at[zz], fm_r.at[zz], dev(3, 0))

    def x_out(zz):
        x_up(zz).start()
        x_down(zz).start()

    def x_pass(zz):
        x_up(zz).wait_recv()
        x_pass_up(zz).start()
        x_down(zz).wait_recv()
        x_pass_down(zz).start()

    def x_step(s):
        x_right(s - 1).wait_recv()
        if s < 8:
            x_right(s).start()
            x_left(s - 1).wait_recv()
            if s < 7:
                x_left(s).start()

    x_right(0).start()
    x_left(0).start()
    tiles[none] = jnp.zeros(tiles.shape[1:], jnp.float32)
    planned.wait()
    own.wait()
    pair.wait()

    def over_y(far, dy):
        return remote(
            packed.at[far, (y + dy) % NY], ybuf.at[far, pl.ds(2 * dy - 2, 2)],
            y_s.at[far, dy - 1], y_r.at[far, dy - 1], dev(dy, 0),
        )

    def pack(far):
        there = (z + far) % NZ
        top = pl.multiple_of(there % 2 * rows, rows)
        for to_y in range(NY):
            for child in range(2):
                index = plan[NZ + child, to_y * (NZ // 2) + there // 2]
                packed[far, to_y, child] = tiles[index, pl.ds(top, rows), :]
        for dy in range(1, NY):
            over_y(far, dy).start()

    def wait_y(far):
        for dy in range(1, NY):
            over_y(far, dy).wait_recv()

    def far_of(way, j):
        return (8 - j if way == 0 else 8 + j) % NZ

    half_list = 4

    def raw_go(way, j):
        far = far_of(way, j)
        to = toward[way]
        dst = (raw1, raw2, raw3)[j]
        mine = packed.at[far, y]
        theirs = ybuf.at[far]
        if j == 0:
            if way == 0:
                pairs = [(mine, pl.ds(0, 2)), (theirs.at[pl.ds(0, 2)], pl.ds(2, 2))]
            else:
                pairs = [(theirs.at[pl.ds(2, 4)], pl.ds(0, 4))]
        else:
            before = (raw1, raw2)[j - 1]
            count = before.shape[1]
            pairs = [(mine, pl.ds(0, 2)), (theirs, pl.ds(2, 6)), (before.at[way], pl.ds(8, count))]
        return [
            remote(a, dst.at[way, b], raw_s.at[way, j, n], raw_r.at[way, j, n], to)
            for n, (a, b) in enumerate(pairs)
        ]

    def cells(g):
        return pl.ds(g * WIDE, WIDE)

    def go(way, j, g):
        return remote(
            dense.at[way, j - 3, cells(g)], dense.at[way, j - 2, cells(g)],
            d_s.at[way, j - 3, g], d_r.at[way, j - 3, g], toward[way],
        )

    def list_cols(far_dest, dz, members):
        there = (z + far_dest) % NZ
        at = (z + dz) % NZ
        return [plan[there // 2 * 2 + child, (y + NY - dy) % NY * NZ + at] for dy, child in members]

    full = [(dy, child) for dy in range(NY) for child in range(2)]

    def own_items(far):
        cols = list_cols(far, 0, full)
        refs = [packed.at[far, y, c] if dy == 0 else ybuf.at[far, 2 * dy - 2 + c] for dy, c in full]
        return list(zip(cols, refs))

    def raw_items(way, far):
        step = NZ - 1 if way == 0 else 1
        last = full[:half_list] if way == 0 else full[half_list:]
        cols = list_cols(far, step, full) + list_cols(far, 2 * step, full) + list_cols(far, 3 * step, last)
        return [(col, raw3.at[way, n]) for n, col in enumerate(cols)]

    def add(total, items, cell):
        for col, ref in items:
            total = total + (col == cell).astype(jnp.float32) * ref[...]
        return total

    def merge(buf, fresh, items, g):
        def one(n, carry):
            cell = g * WIDE + n
            start = jnp.zeros(buf.shape[1:], jnp.float32) if fresh else buf[cell]
            buf[cell] = add(start, items, cell)
            return carry

        lax.fori_loop(0, WIDE, one, 0)

    def strip(body):
        def one(n, carry):
            body(pl.ds(pl.multiple_of(n * SUB, SUB), SUB), n * SUB)
            return carry

        lax.fori_loop(0, lead // SUB, one, 0)

    def places(start, shape):
        row = lax.broadcasted_iota(jnp.int32, shape, 0) + start
        col = lax.broadcasted_iota(jnp.int32, shape, 1)
        return row, col

    def load_lead():
        for zz in range(8):
            x_pass_up(zz).wait_recv()
            x_pass_down(zz).wait_recv()

        def rows_of(at, start):
            block = xbuf[pl.ds(start // rows, SUB // rows)].reshape(SUB, lead)
            lead_ref[at, :] = block
            a_hi[at, :], a_lo[at, :] = split(block)

        strip(rows_of)

    def keep_m(at, value):
        m_ref[at, :] = value
        m_hi[at, :], m_lo[at, :] = split(value)

    def begin():
        def diagonal(at, start):
            row, col = places(start, (SUB, lead))
            t_ref[at, :] = jnp.where(row == col, lead_ref[at, :], 0.0)

        strip(diagonal)
        across = lax.rsqrt(jnp.sum(t_ref[...], axis=0, keepdims=True))

        def rows_of(at, start):
            row, col = places(start, (SUB, lead))
            down = lax.rsqrt(jnp.sum(t_ref[at, :], axis=1, keepdims=True))
            lower = jnp.where(row > col, lead_ref[at, :] * down, 0.0)
            unit = (row == col).astype(jnp.float32)
            diag = jnp.where(row == col, lead_ref[at, :], 0.0) * down * across
            keep_m(at, (unit - lower * across - 0.5 * (diag - unit)) * across)

        strip(rows_of)

    def round_of(exact):
        def pair(high, low):
            return (high, low) if exact else (high,)

        def product(left, right, dims):
            return dot3(left, right, dims) if exact else dot1(left[0], right[0], dims)

        def each(body):
            for n in range(lead // SUB):
                body(pl.ds(n * SUB, SUB), pl.ds(0, (n + 1) * SUB), n * SUB)

        def round_a():
            def rows_of(at, upto, start):
                left = pair(m_hi[at, upto], m_lo[at, upto])
                t_ref[at, upto] = product(left, pair(a_hi[upto, upto], a_lo[upto, upto]), NN)

            each(rows_of)

        def round_b():
            def rows_of(at, upto, start):
                gap = product(split(t_ref[at, upto]), pair(m_hi[upto, upto], m_lo[upto, upto]), NT)
                row, col = places(start, gap.shape)
                g_ref[at, upto] = jnp.where(row > col, gap, jnp.where(row == col, 0.5 * (gap - 1.0), 0.0))

            each(rows_of)

        def round_c():
            def rows_of(at, upto, start):
                fix = product(split(g_ref[at, upto]), pair(m_hi[upto, upto], m_lo[upto, upto]), NN)
                t_ref[at, upto] = m_ref[at, upto] - fix

            each(rows_of)

            def keep(at, upto, start):
                value = t_ref[at, upto]
                m_ref[at, upto] = value
                m_hi[at, upto], m_lo[at, upto] = split(value)

            each(keep)

        return [round_a, round_b, round_c]

    def weigh():
        inverse = (m_hi[...], m_lo[...])
        row, col = places(me * rows, (rows, lead))
        value = dot3(split(xbuf[me]), inverse, NT)
        value = jnp.where(col <= row, value, 0.0)
        out_ref[0, :, :lead] = value
        value = jnp.where(col < row // tile * tile, value, 0.0)
        w_hi[...], w_lo[...] = split(dot3(split(value), inverse, NN))

    def rest_panels():
        for zz in range(8, NZ):
            x_pass_up(zz).wait_recv()
            x_pass_down(zz).wait_recv()

    def subtract(g):
        weights = (w_hi[...], w_lo[...])

        def one(n, carry):
            cell = g * WIDE + n
            block = xbuf[pl.ds(lead // rows + tile // rows * cell, tile // rows)].reshape(tile, lead)
            at = pl.ds(pl.multiple_of(lead + cell * tile, tile), tile)
            out_ref[0, :, at] = -dot3(weights, split(block), NT)
            return carry

        lax.fori_loop(0, WIDE, one, 0)

    todo = [load_lead, begin]
    for n in range(1, ROUNDS):
        todo += round_of(n > COARSE)
    todo += [weigh, rest_panels] + [lambda g=g: subtract(g) for g in range(CHUNKS)]

    def work(count):
        for _ in range(count):
            if todo:
                todo.pop(0)()

    def raw_start(way, j, own):
        copies = raw_go(way, j)
        count = len(copies) if j == 0 else 2
        for copy in copies[:count] if own else copies[count:]:
            copy.start()

    def raw_recv(j):
        for way in range(2):
            for copy in raw_go(way, j):
                copy.wait_recv()

    def raw_own(j):
        for way in range(2):
            wait_y(far_of(way, j))
            raw_start(way, j, True)

    def raw_forward(j):
        raw_recv(j - 1)
        for way in range(2):
            raw_start(way, j, False)

    def packs(*members):
        for far in members:
            pack(far)

    packs(8)
    x_step(1)
    packs(7, 9)
    wait_y(8)
    for way in range(2):
        raw_start(way, 0, True)
    packs(6, 10)
    x_step(2)
    raw_own(1)
    packs(5, 11)
    x_step(3)
    raw_forward(1)
    packs(4, 12)
    x_step(4)
    raw_own(2)
    packs(3, 13)
    x_step(5)
    raw_forward(2)
    packs(2, 14)
    x_step(6)
    packs(1, 15, 0)
    raw_recv(2)
    for way in range(2):
        wait_y(far_of(way, 3))
    items = [own_items(far_of(way, 3)) + raw_items(way, far_of(way, 3)) for way in range(2)]
    for g in range(CHUNKS):
        for way in range(2):
            merge(dense.at[way, 0], True, items[way], g)
            go(way, 3, g).start()
        if g == 1:
            x_step(7)
    x_step(8)
    for zz in range(8):
        x_out(zz)
    outs, passes = list(range(8, NZ)), list(range(NZ))
    for j in range(4, 8):
        for way in range(2):
            wait_y(far_of(way, j))
        items = [own_items(far_of(way, j)) for way in range(2)]
        for g in range(CHUNKS):
            for way in range(2):
                go(way, j - 1, g).wait_recv()
                merge(dense.at[way, j - 3], False, items[way], g)
                go(way, j, g).start()
            slot_at = (j - 4) * CHUNKS + g
            if slot_at > 0:
                for zz in passes[:2]:
                    x_pass(zz)
                del passes[:2]
                for zz in outs[:2]:
                    x_out(zz)
                del outs[:2]
            if slot_at > 5:
                work(2 if slot_at < 12 else 3)

    while todo:
        work(1)
    wait_y(0)
    items = own_items(0)
    for g in range(CHUNKS):
        for way in range(2):
            go(way, 7, g).wait_recv()

        def last(n, carry):
            cell = g * WIDE + n
            at = pl.ds(pl.multiple_of(lead + cell * tile, tile), tile)
            total = add(dense[0, 5, cell] + dense[1, 5, cell], items, cell)
            out_ref[0, :, at] = out_ref[0, :, at] + total
            return carry

        lax.fori_loop(0, WIDE, last, 0)

    for zz in range(NZ):
        for copy in (x_up(zz), x_down(zz), x_pass_up(zz), x_pass_down(zz)):
            copy.wait_send()
        for dy in range(1, NY):
            over_y(zz, dy).wait_send()
    for s in range(8):
        x_right(s).wait_send()
        if s < 7:
            x_left(s).wait_send()
    for way in range(2):
        for j in range(3):
            for copy in raw_go(way, j):
                copy.wait_send()
        for j in range(3, 8):
            for g in range(CHUNKS):
                go(way, j, g).wait_send()


def exchange(front, own_tiles, partner_tiles, tile_rows, tile_cols, live, lead):
    rows = front.shape[1]
    tile = own_tiles.shape[-1]
    slots = own_tiles.shape[1]
    sem = pltpu.SemaphoreType.DMA
    any_spec = pl.BlockSpec(memory_space=pl.ANY)
    vmem = pl.BlockSpec(memory_space=pltpu.VMEM)
    f32, bf16 = jnp.float32, jnp.bfloat16
    return pl.pallas_call(
        exchange_kernel,
        out_shape=jax.ShapeDtypeStruct(front.shape, f32),
        in_specs=[any_spec, any_spec, any_spec, vmem, vmem, vmem],
        out_specs=vmem,
        scratch_shapes=[
            pltpu.VMEM((2 * slots + 1, tile, tile), f32),
            pltpu.VMEM((NZ, NY, 2, rows, tile), f32),
            pltpu.VMEM((NZ, 2 * NY - 2, rows, tile), f32),
            pltpu.VMEM((2, 4, rows, tile), f32),
            pltpu.VMEM((2, 12, rows, tile), f32),
            pltpu.VMEM((2, 20, rows, tile), f32),
            pltpu.VMEM((2, 6, CELLS, rows, tile), f32),
            pltpu.VMEM((NY * NZ, rows, lead), f32),
        ]
        + [pltpu.VMEM((24, 128), jnp.int32), pltpu.SMEM((24, 128), jnp.int32)]
        + [pltpu.VMEM((lead, lead), f32)] * 4
        + [pltpu.VMEM((lead, lead), bf16)] * 4
        + [pltpu.VMEM((rows, lead), bf16)] * 2
        + [
            sem((3,)), sem, sem,
            sem((NZ, NY - 1)), sem((NZ, NY - 1)),
            sem((2, 3, 3)), sem((2, 3, 3)),
            sem((2, 5, CHUNKS)), sem((2, 5, CHUNKS)),
            sem((8,)), sem((8,)), sem((7,)), sem((7,)),
        ] + [sem((NZ,))] * 8,
        compiler_params=pltpu.CompilerParams(
            collective_id=0, has_side_effects=True, vmem_limit_bytes=56 * 2**20
        ),
    )(front, own_tiles, partner_tiles, tile_rows, tile_cols, live)


def body(front, own_tiles, partner_tiles, tile_rows, tile_cols, live):
    lead = PANELS * own_tiles.shape[-1]
    tile_rows = tile_rows[:, :, :, 0].transpose(0, 2, 1)
    tile_cols = tile_cols.transpose(0, 2, 1)
    live = live.transpose(0, 2, 1)
    change = exchange(front, own_tiles, partner_tiles, tile_rows, tile_cols, live, lead)
    factored = lax.broadcasted_iota(jnp.int32, change.shape, 2) < lead
    return jnp.where(factored, change, change + front)


def solution(mesh):
    in_specs = (
        P("front", "cube", None),
        P("front", "cube", None, None),
        P("front", "cube", None, None),
        P(),
        P(),
        P(),
    )
    out_specs = P("front", "cube", None)
    return jax.shard_map(body, mesh=mesh, in_specs=in_specs, out_specs=out_specs, check_vma=False)
```

```python
import jax
import jax.numpy as jnp
from jax import lax
from jax.experimental import pallas as pl
from jax.experimental.pallas import tpu as pltpu
from jax.sharding import PartitionSpec as P

PANELS = 4
NY = 4
NZ = 16
CELLS = 28
CHUNKS = 4
WIDE = CELLS // CHUNKS
ROUNDS = 6
COARSE = 2
SUB = 128
MESH = pl.DeviceIdType.MESH
NN = (((1,), (0,)), ((), ()))
NT = (((1,), (1,)), ((), ()))


def split(value):
    high = value.astype(jnp.bfloat16)
    return high, (value - high.astype(jnp.float32)).astype(jnp.bfloat16)


def dot1(left, right, dims):
    return lax.dot_general(left, right, dims, preferred_element_type=jnp.float32)


def dot3(left, right, dims):
    small = dot1(left[0], right[1], dims) + dot1(left[1], right[0], dims)
    return small + dot1(left[0], right[0], dims)


def fill_table(table, rows_ref, cols_ref, live_ref, side, y, me, slots):
    devices = rows_ref.shape[2]
    table[...] = jnp.zeros(table.shape, jnp.int32)
    spot = lax.broadcasted_iota(jnp.int32, (slots, devices), 0)
    lane = lax.broadcasted_iota(jnp.int32, (slots, devices), 1)
    wide_spot = lax.broadcasted_iota(jnp.int32, (slots, 128), 0)
    wide_lane = lax.broadcasted_iota(jnp.int32, (slots, 128), 1)
    for child in range(2):
        at = pl.ds(child * slots, slots)
        alive = spot < live_ref[side, pl.ds(child, 1), :]
        rows = jnp.where(alive, rows_ref[side, at, :], -1)
        cells = cols_ref[side, at, :] - (PANELS - 1)
        for q in range(NZ // 2):
            hit = rows == y * (NZ // 2) + q
            found = jnp.sum(jnp.where(hit, cells, 0), axis=0, keepdims=True) - 1
            table[pl.ds(2 * q + child, 1), pl.ds(0, devices)] = found
        mine = jnp.sum(jnp.where(lane == me, rows, 0), axis=1, keepdims=True)
        slot = wide_spot + (child * slots - 2 * slots)
        found = jnp.sum(jnp.where(mine == wide_lane, slot, 0), axis=0, keepdims=True)
        table[pl.ds(NZ + child, 1), :] = found + 2 * slots


def exchange_kernel(
    front_ref, own_ref, partner_ref, rows_ref, cols_ref, live_ref, out_ref,
    tiles, packed, ybuf, raw1, raw2, raw3, dense, xbuf,
    table, plan, lead_ref, m_ref, t_ref, g_ref, a_hi, a_lo, m_hi, m_lo, w_hi, w_lo,
    load_sem, pair_s, pair_r, y_s, y_r, raw_s, raw_r, d_s, d_r,
    zr_s, zr_r, zl_s, zl_r, yp_s, yp_r, ym_s, ym_r, fp_s, fp_r, fm_s, fm_r,
):
    me = lax.axis_index("cube")
    side = lax.axis_index("front")
    y, z = me // NZ, me % NZ
    rows, lead = xbuf.shape[1], xbuf.shape[2]
    slots = own_ref.shape[1]
    none = 2 * slots
    tile = tiles.shape[1]

    def dev(dy, dz):
        return {"cube": (y + dy) % NY * NZ + (z + dz) % NZ}

    mate = {"front": side + 1 - 2 * (side % 2)}
    toward = [dev(0, 1), dev(0, NZ - 1)]
    peers = toward + [dev(1, 0), dev(2, 0), dev(3, 0), mate]
    barrier = pltpu.get_barrier_semaphore()
    for peer in peers:
        pl.semaphore_signal(barrier, inc=1, device_id=peer, device_id_type=MESH)
    mine = pltpu.make_async_copy(front_ref.at[0, :, pl.ds(0, lead)], xbuf.at[me], load_sem.at[1])
    mine.start()
    own = pltpu.make_async_copy(own_ref.at[0], tiles.at[pl.ds(0, slots)], load_sem.at[0])
    own.start()
    fill_table(table, rows_ref, cols_ref, live_ref, side, y, me, slots)
    planned = pltpu.make_async_copy(table, plan, load_sem.at[2])
    planned.start()
    pl.semaphore_wait(barrier, len(peers))

    def remote(src, dst, send, recv, to):
        return pltpu.make_async_remote_copy(
            src_ref=src, dst_ref=dst, send_sem=send, recv_sem=recv, device_id=to, device_id_type=MESH
        )

    pair = remote(partner_ref.at[0], tiles.at[pl.ds(slots, slots)], pair_s, pair_r, mate)
    pair.start()
    mine.wait()

    def slot(dy, zz):
        return xbuf.at[(y + dy) % NY * NZ + zz]

    def x_right(s):
        ref = slot(0, (z + NZ - s) % NZ)
        return remote(ref, ref, zr_s.at[s], zr_r.at[s], toward[0])

    def x_left(s):
        ref = slot(0, (z + s) % NZ)
        return remote(ref, ref, zl_s.at[s], zl_r.at[s], toward[1])

    def x_up(zz):
        ref = slot(0, zz)
        return remote(ref, ref, yp_s.at[zz], yp_r.at[zz], dev(1, 0))

    def x_down(zz):
        ref = slot(0, zz)
        return remote(ref, ref, ym_s.at[zz], ym_r.at[zz], dev(3, 0))

    def x_pass_up(zz):
        ref = slot(3, zz).at[pl.ds(0, rows // 2)]
        return remote(ref, ref, fp_s.at[zz], fp_r.at[zz], dev(1, 0))

    def x_pass_down(zz):
        ref = slot(1, zz).at[pl.ds(rows // 2, rows // 2)]
        return remote(ref, ref, fm_s.at[zz], fm_r.at[zz], dev(3, 0))

    def x_out(zz):
        x_up(zz).start()
        x_down(zz).start()

    def x_pass(zz):
        x_up(zz).wait_recv()
        x_pass_up(zz).start()
        x_down(zz).wait_recv()
        x_pass_down(zz).start()

    def x_step(s):
        x_right(s - 1).wait_recv()
        if s < 8:
            x_right(s).start()
            x_left(s - 1).wait_recv()
            if s < 7:
                x_left(s).start()

    x_right(0).start()
    x_left(0).start()
    tiles[none] = jnp.zeros(tiles.shape[1:], jnp.float32)
    planned.wait()
    x_step(1)
    own.wait()
    pair.wait()

    def over_y(far, dy):
        return remote(
            packed.at[far, (y + dy) % NY], ybuf.at[far, pl.ds(2 * dy - 2, 2)],
            y_s.at[far, dy - 1], y_r.at[far, dy - 1], dev(dy, 0),
        )

    def pack(far):
        there = (z + far) % NZ
        top = pl.multiple_of(there % 2 * rows, rows)
        for to_y in range(NY):
            for child in range(2):
                index = plan[NZ + child, to_y * (NZ // 2) + there // 2]
                packed[far, to_y, child] = tiles[index, pl.ds(top, rows), :]
        for dy in range(1, NY):
            over_y(far, dy).start()

    def wait_y(far):
        for dy in range(1, NY):
            over_y(far, dy).wait_recv()

    def far_of(way, j):
        return (8 - j if way == 0 else 8 + j) % NZ

    half_list = 4

    def raw_go(way, j):
        far = far_of(way, j)
        to = toward[way]
        dst = (raw1, raw2, raw3)[j]
        mine = packed.at[far, y]
        theirs = ybuf.at[far]
        if j == 0:
            if way == 0:
                pairs = [(mine, pl.ds(0, 2)), (theirs.at[pl.ds(0, 2)], pl.ds(2, 2))]
            else:
                pairs = [(theirs.at[pl.ds(2, 4)], pl.ds(0, 4))]
        else:
            before = (raw1, raw2)[j - 1]
            count = before.shape[1]
            pairs = [(mine, pl.ds(0, 2)), (theirs, pl.ds(2, 6)), (before.at[way], pl.ds(8, count))]
        return [
            remote(a, dst.at[way, b], raw_s.at[way, j, n], raw_r.at[way, j, n], to)
            for n, (a, b) in enumerate(pairs)
        ]

    def cells(g):
        return pl.ds(g * WIDE, WIDE)

    def go(way, j, g):
        return remote(
            dense.at[way, j - 3, cells(g)], dense.at[way, j - 2, cells(g)],
            d_s.at[way, j - 3, g], d_r.at[way, j - 3, g], toward[way],
        )

    def list_cols(far_dest, dz, members):
        there = (z + far_dest) % NZ
        at = (z + dz) % NZ
        return [plan[there // 2 * 2 + child, (y + NY - dy) % NY * NZ + at] for dy, child in members]

    full = [(dy, child) for dy in range(NY) for child in range(2)]

    def own_items(far):
        cols = list_cols(far, 0, full)
        refs = [packed.at[far, y, c] if dy == 0 else ybuf.at[far, 2 * dy - 2 + c] for dy, c in full]
        return list(zip(cols, refs))

    def raw_items(way, far):
        step = NZ - 1 if way == 0 else 1
        last = full[:half_list] if way == 0 else full[half_list:]
        cols = list_cols(far, step, full) + list_cols(far, 2 * step, full) + list_cols(far, 3 * step, last)
        return [(col, raw3.at[way, n]) for n, col in enumerate(cols)]

    def add(total, items, cell):
        for col, ref in items:
            total = total + (col == cell).astype(jnp.float32) * ref[...]
        return total

    def merge(buf, fresh, items, g):
        def one(n, carry):
            cell = g * WIDE + n
            start = jnp.zeros(buf.shape[1:], jnp.float32) if fresh else buf[cell]
            buf[cell] = add(start, items, cell)
            return carry

        lax.fori_loop(0, WIDE, one, 0)

    def strip(body):
        def one(n, carry):
            body(pl.ds(pl.multiple_of(n * SUB, SUB), SUB), n * SUB)
            return carry

        lax.fori_loop(0, lead // SUB, one, 0)

    def places(start, shape):
        row = lax.broadcasted_iota(jnp.int32, shape, 0) + start
        col = lax.broadcasted_iota(jnp.int32, shape, 1)
        return row, col

    def load_lead():
        for zz in range(8):
            x_pass_up(zz).wait_recv()
            x_pass_down(zz).wait_recv()

        def rows_of(at, start):
            block = xbuf[pl.ds(start // rows, SUB // rows)].reshape(SUB, lead)
            lead_ref[at, :] = block
            a_hi[at, :], a_lo[at, :] = split(block)

        strip(rows_of)

    def keep_m(at, value):
        m_ref[at, :] = value
        m_hi[at, :], m_lo[at, :] = split(value)

    def begin():
        def diagonal(at, start):
            row, col = places(start, (SUB, lead))
            t_ref[at, :] = jnp.where(row == col, lead_ref[at, :], 0.0)

        strip(diagonal)
        across = lax.rsqrt(jnp.sum(t_ref[...], axis=0, keepdims=True))

        def rows_of(at, start):
            row, col = places(start, (SUB, lead))
            down = lax.rsqrt(jnp.sum(t_ref[at, :], axis=1, keepdims=True))
            lower = jnp.where(row > col, lead_ref[at, :] * down, 0.0)
            unit = (row == col).astype(jnp.float32)
            diag = jnp.where(row == col, lead_ref[at, :], 0.0) * down * across
            keep_m(at, (unit - lower * across - 0.5 * (diag - unit)) * across)

        strip(rows_of)

    def round_of(exact):
        def pair(high, low):
            return (high, low) if exact else (high,)

        def product(left, right, dims):
            return dot3(left, right, dims) if exact else dot1(left[0], right[0], dims)

        def each(body):
            for n in range(lead // SUB):
                body(pl.ds(n * SUB, SUB), pl.ds(0, (n + 1) * SUB), n * SUB)

        def round_a():
            def rows_of(at, upto, start):
                left = pair(m_hi[at, upto], m_lo[at, upto])
                t_ref[at, upto] = product(left, pair(a_hi[upto, upto], a_lo[upto, upto]), NN)

            each(rows_of)

        def round_b():
            def rows_of(at, upto, start):
                gap = product(split(t_ref[at, upto]), pair(m_hi[upto, upto], m_lo[upto, upto]), NT)
                row, col = places(start, gap.shape)
                g_ref[at, upto] = jnp.where(row > col, gap, jnp.where(row == col, 0.5 * (gap - 1.0), 0.0))

            each(rows_of)

        def round_c():
            def rows_of(at, upto, start):
                fix = product(split(g_ref[at, upto]), pair(m_hi[upto, upto], m_lo[upto, upto]), NN)
                t_ref[at, upto] = m_ref[at, upto] - fix

            each(rows_of)

            def keep(at, upto, start):
                value = t_ref[at, upto]
                m_ref[at, upto] = value
                m_hi[at, upto], m_lo[at, upto] = split(value)

            each(keep)

        return [round_a, round_b, round_c]

    def weigh():
        inverse = (m_hi[...], m_lo[...])
        row, col = places(me * rows, (rows, lead))
        value = dot3(split(xbuf[me]), inverse, NT)
        value = jnp.where(col <= row, value, 0.0)
        out_ref[0, :, :lead] = value
        value = jnp.where(col < row // tile * tile, value, 0.0)
        w_hi[...], w_lo[...] = split(dot3(split(value), inverse, NN))

    def rest_panels():
        for zz in range(8, NZ):
            x_pass_up(zz).wait_recv()
            x_pass_down(zz).wait_recv()

    def subtract(g):
        weights = (w_hi[...], w_lo[...])

        def one(n, carry):
            cell = g * WIDE + n
            block = xbuf[pl.ds(lead // rows + tile // rows * cell, tile // rows)].reshape(tile, lead)
            at = pl.ds(pl.multiple_of(lead + cell * tile, tile), tile)
            out_ref[0, :, at] = -dot3(weights, split(block), NT)
            return carry

        lax.fori_loop(0, WIDE, one, 0)

    todo = [load_lead, begin]
    for n in range(1, ROUNDS):
        todo += round_of(n > COARSE)
    todo += [weigh, rest_panels] + [lambda g=g: subtract(g) for g in range(CHUNKS)]

    def work(count):
        for _ in range(count):
            if todo:
                todo.pop(0)()

    def raw_start(way, j, own):
        copies = raw_go(way, j)
        count = len(copies) if j == 0 else 2
        for copy in copies[:count] if own else copies[count:]:
            copy.start()

    def raw_own(j):
        for way in range(2):
            wait_y(far_of(way, j))
            raw_start(way, j, True)

    def raw_forward(j):
        for way in range(2):
            for copy in raw_go(way, j - 1):
                copy.wait_recv()
        for way in range(2):
            raw_start(way, j, False)

    def packs(*members):
        for far in members:
            pack(far)

    packs(8, 7, 9)
    x_step(2)
    wait_y(8)
    for way in range(2):
        raw_start(way, 0, True)
    packs(6, 10)
    x_step(3)
    raw_own(1)
    packs(5, 11)
    x_step(4)
    raw_forward(1)
    packs(4, 12)
    x_step(5)
    raw_own(2)
    packs(3, 13)
    x_step(6)
    raw_forward(2)
    packs(2, 14, 1, 15, 0)
    later = []
    for way in range(2):
        far = far_of(way, 3)
        wait_y(far)
        for copy in raw_go(way, 2)[:2]:
            copy.wait_recv()
        lists = raw_items(way, far)
        later.append(lists[8:])
        for g in range(CHUNKS):
            merge(dense.at[way, 0], True, own_items(far) + lists[:8], g)
    x_step(7)
    for way in range(2):
        raw_go(way, 2)[2].wait_recv()
    for g in range(CHUNKS):
        for way in range(2):
            merge(dense.at[way, 0], False, later[way], g)
            go(way, 3, g).start()
        if g == 1:
            x_step(8)
            for zz in range(8):
                x_out(zz)
    outs, passes = list(range(8, NZ)), list(range(NZ))
    for j in range(4, 8):
        for way in range(2):
            wait_y(far_of(way, j))
        items = [own_items(far_of(way, j)) for way in range(2)]
        for g in range(CHUNKS):
            for way in range(2):
                go(way, j - 1, g).wait_recv()
                merge(dense.at[way, j - 3], False, items[way], g)
                go(way, j, g).start()
            slot_at = (j - 4) * CHUNKS + g
            for zz in passes[:2]:
                x_pass(zz)
            del passes[:2]
            for zz in outs[:2]:
                x_out(zz)
            del outs[:2]
            if slot_at > 4:
                work(2 if slot_at < 14 else 3)

    while todo:
        work(1)
    wait_y(0)
    items = own_items(0)
    for g in range(CHUNKS):
        for way in range(2):
            go(way, 7, g).wait_recv()

        def last(n, carry):
            cell = g * WIDE + n
            at = pl.ds(pl.multiple_of(lead + cell * tile, tile), tile)
            total = add(dense[0, 5, cell] + dense[1, 5, cell], items, cell)
            out_ref[0, :, at] = out_ref[0, :, at] + total
            return carry

        lax.fori_loop(0, WIDE, last, 0)

    for zz in range(NZ):
        for copy in (x_up(zz), x_down(zz), x_pass_up(zz), x_pass_down(zz)):
            copy.wait_send()
        for dy in range(1, NY):
            over_y(zz, dy).wait_send()
    for s in range(8):
        x_right(s).wait_send()
        if s < 7:
            x_left(s).wait_send()
    for way in range(2):
        for j in range(3):
            for copy in raw_go(way, j):
                copy.wait_send()
        for j in range(3, 8):
            for g in range(CHUNKS):
                go(way, j, g).wait_send()


def exchange(front, own_tiles, partner_tiles, tile_rows, tile_cols, live, lead):
    rows = front.shape[1]
    tile = own_tiles.shape[-1]
    slots = own_tiles.shape[1]
    sem = pltpu.SemaphoreType.DMA
    any_spec = pl.BlockSpec(memory_space=pl.ANY)
    vmem = pl.BlockSpec(memory_space=pltpu.VMEM)
    f32, bf16 = jnp.float32, jnp.bfloat16
    return pl.pallas_call(
        exchange_kernel,
        out_shape=jax.ShapeDtypeStruct(front.shape, f32),
        in_specs=[any_spec, any_spec, any_spec, vmem, vmem, vmem],
        out_specs=vmem,
        scratch_shapes=[
            pltpu.VMEM((2 * slots + 1, tile, tile), f32),
            pltpu.VMEM((NZ, NY, 2, rows, tile), f32),
            pltpu.VMEM((NZ, 2 * NY - 2, rows, tile), f32),
            pltpu.VMEM((2, 4, rows, tile), f32),
            pltpu.VMEM((2, 12, rows, tile), f32),
            pltpu.VMEM((2, 20, rows, tile), f32),
            pltpu.VMEM((2, 6, CELLS, rows, tile), f32),
            pltpu.VMEM((NY * NZ, rows, lead), f32),
        ]
        + [pltpu.VMEM((24, 128), jnp.int32), pltpu.SMEM((24, 128), jnp.int32)]
        + [pltpu.VMEM((lead, lead), f32)] * 4
        + [pltpu.VMEM((lead, lead), bf16)] * 4
        + [pltpu.VMEM((rows, lead), bf16)] * 2
        + [
            sem((3,)), sem, sem,
            sem((NZ, NY - 1)), sem((NZ, NY - 1)),
            sem((2, 3, 3)), sem((2, 3, 3)),
            sem((2, 5, CHUNKS)), sem((2, 5, CHUNKS)),
            sem((8,)), sem((8,)), sem((7,)), sem((7,)),
        ] + [sem((NZ,))] * 8,
        compiler_params=pltpu.CompilerParams(
            collective_id=0, has_side_effects=True, vmem_limit_bytes=56 * 2**20
        ),
    )(front, own_tiles, partner_tiles, tile_rows, tile_cols, live)


def body(front, own_tiles, partner_tiles, tile_rows, tile_cols, live):
    lead = PANELS * own_tiles.shape[-1]
    tile_rows = tile_rows[:, :, :, 0].transpose(0, 2, 1)
    tile_cols = tile_cols.transpose(0, 2, 1)
    live = live.transpose(0, 2, 1)
    change = exchange(front, own_tiles, partner_tiles, tile_rows, tile_cols, live, lead)
    factored = lax.broadcasted_iota(jnp.int32, change.shape, 2) < lead
    return jnp.where(factored, change, change + front)


def solution(mesh):
    in_specs = (
        P("front", "cube", None),
        P("front", "cube", None, None),
        P("front", "cube", None, None),
        P(),
        P(),
        P(),
    )
    out_specs = P("front", "cube", None)
    return jax.shard_map(body, mesh=mesh, in_specs=in_specs, out_specs=out_specs, check_vma=False)
```

```python
import jax
import jax.numpy as jnp
from jax import lax
from jax.experimental import pallas as pl
from jax.experimental.pallas import tpu as pltpu
from jax.sharding import PartitionSpec as P

PANELS = 4
NY = 4
NZ = 16
CELLS = 28
CHUNKS = 4
WIDE = CELLS // CHUNKS
ROUNDS = 6
COARSE = 2
SUB = 128
MESH = pl.DeviceIdType.MESH
NN = (((1,), (0,)), ((), ()))
NT = (((1,), (1,)), ((), ()))


def split(value):
    high = value.astype(jnp.bfloat16)
    return high, (value - high.astype(jnp.float32)).astype(jnp.bfloat16)


def dot1(left, right, dims):
    return lax.dot_general(left, right, dims, preferred_element_type=jnp.float32)


def dot3(left, right, dims):
    small = dot1(left[0], right[1], dims) + dot1(left[1], right[0], dims)
    return small + dot1(left[0], right[0], dims)


def fill_table(table, rows_ref, cols_ref, live_ref, side, y, me, slots):
    devices = rows_ref.shape[2]
    table[...] = jnp.zeros(table.shape, jnp.int32)
    spot = lax.broadcasted_iota(jnp.int32, (slots, devices), 0)
    lane = lax.broadcasted_iota(jnp.int32, (slots, devices), 1)
    wide_spot = lax.broadcasted_iota(jnp.int32, (slots, 128), 0)
    wide_lane = lax.broadcasted_iota(jnp.int32, (slots, 128), 1)
    for child in range(2):
        at = pl.ds(child * slots, slots)
        alive = spot < live_ref[side, pl.ds(child, 1), :]
        rows = jnp.where(alive, rows_ref[side, at, :], -1)
        cells = cols_ref[side, at, :] - (PANELS - 1)
        for q in range(NZ // 2):
            hit = rows == y * (NZ // 2) + q
            found = jnp.sum(jnp.where(hit, cells, 0), axis=0, keepdims=True) - 1
            table[pl.ds(2 * q + child, 1), pl.ds(0, devices)] = found
        mine = jnp.sum(jnp.where(lane == me, rows, 0), axis=1, keepdims=True)
        slot = wide_spot + (child * slots - 2 * slots)
        found = jnp.sum(jnp.where(mine == wide_lane, slot, 0), axis=0, keepdims=True)
        table[pl.ds(NZ + child, 1), :] = found + 2 * slots


def exchange_kernel(
    front_ref, own_ref, partner_ref, rows_ref, cols_ref, live_ref, out_ref,
    tiles, packed, ybuf, raw1, raw2, raw3, dense, xbuf,
    table, plan, lead_ref, m_ref, t_ref, g_ref, a_hi, a_lo, m_hi, m_lo, w_hi, w_lo,
    load_sem, pair_s, pair_r, y_s, y_r, raw_s, raw_r, d_s, d_r,
    zr_s, zr_r, zl_s, zl_r, yp_s, yp_r, ym_s, ym_r, fp_s, fp_r, fm_s, fm_r,
):
    me = lax.axis_index("cube")
    side = lax.axis_index("front")
    y, z = me // NZ, me % NZ
    rows, lead = xbuf.shape[1], xbuf.shape[2]
    slots = own_ref.shape[1]
    none = 2 * slots
    tile = tiles.shape[1]

    def dev(dy, dz):
        return {"cube": (y + dy) % NY * NZ + (z + dz) % NZ}

    mate = {"front": side + 1 - 2 * (side % 2)}
    toward = [dev(0, 1), dev(0, NZ - 1)]
    peers = toward + [dev(1, 0), dev(2, 0), dev(3, 0), mate]
    barrier = pltpu.get_barrier_semaphore()
    for peer in peers:
        pl.semaphore_signal(barrier, inc=1, device_id=peer, device_id_type=MESH)
    mine = pltpu.make_async_copy(front_ref.at[0, :, pl.ds(0, lead)], xbuf.at[me], load_sem.at[1])
    mine.start()
    own = pltpu.make_async_copy(own_ref.at[0], tiles.at[pl.ds(0, slots)], load_sem.at[0])
    own.start()
    fill_table(table, rows_ref, cols_ref, live_ref, side, y, me, slots)
    planned = pltpu.make_async_copy(table, plan, load_sem.at[2])
    planned.start()
    pl.semaphore_wait(barrier, len(peers))

    def remote(src, dst, send, recv, to):
        return pltpu.make_async_remote_copy(
            src_ref=src, dst_ref=dst, send_sem=send, recv_sem=recv, device_id=to, device_id_type=MESH
        )

    pair = remote(partner_ref.at[0], tiles.at[pl.ds(slots, slots)], pair_s, pair_r, mate)
    pair.start()
    mine.wait()

    def slot(dy, zz):
        return xbuf.at[(y + dy) % NY * NZ + zz]

    def x_right(s):
        ref = slot(0, (z + NZ - s) % NZ)
        return remote(ref, ref, zr_s.at[s], zr_r.at[s], toward[0])

    def x_left(s):
        ref = slot(0, (z + s) % NZ)
        return remote(ref, ref, zl_s.at[s], zl_r.at[s], toward[1])

    def x_up(zz):
        ref = slot(0, zz)
        return remote(ref, ref, yp_s.at[zz], yp_r.at[zz], dev(1, 0))

    def x_down(zz):
        ref = slot(0, zz)
        return remote(ref, ref, ym_s.at[zz], ym_r.at[zz], dev(3, 0))

    def x_pass_up(zz):
        ref = slot(3, zz).at[pl.ds(0, rows // 2)]
        return remote(ref, ref, fp_s.at[zz], fp_r.at[zz], dev(1, 0))

    def x_pass_down(zz):
        ref = slot(1, zz).at[pl.ds(rows // 2, rows // 2)]
        return remote(ref, ref, fm_s.at[zz], fm_r.at[zz], dev(3, 0))

    def x_out(zz):
        x_up(zz).start()
        x_down(zz).start()

    def x_pass(zz):
        x_up(zz).wait_recv()
        x_pass_up(zz).start()
        x_down(zz).wait_recv()
        x_pass_down(zz).start()

    def x_step(s):
        x_right(s - 1).wait_recv()
        if s < 8:
            x_right(s).start()
            x_left(s - 1).wait_recv()
            if s < 7:
                x_left(s).start()

    x_right(0).start()
    x_left(0).start()
    tiles[none] = jnp.zeros(tiles.shape[1:], jnp.float32)
    planned.wait()
    x_step(1)
    own.wait()
    pair.wait()

    def over_y(far, dy):
        return remote(
            packed.at[far, (y + dy) % NY], ybuf.at[far, pl.ds(2 * dy - 2, 2)],
            y_s.at[far, dy - 1], y_r.at[far, dy - 1], dev(dy, 0),
        )

    def pack(far):
        there = (z + far) % NZ
        top = pl.multiple_of(there % 2 * rows, rows)
        for to_y in range(NY):
            for child in range(2):
                index = plan[NZ + child, to_y * (NZ // 2) + there // 2]
                packed[far, to_y, child] = tiles[index, pl.ds(top, rows), :]
        for dy in range(1, NY):
            over_y(far, dy).start()

    def wait_y(far):
        for dy in range(1, NY):
            over_y(far, dy).wait_recv()

    def far_of(way, j):
        return (8 - j if way == 0 else 8 + j) % NZ

    half_list = 4

    def raw_go(way, j):
        far = far_of(way, j)
        to = toward[way]
        dst = (raw1, raw2, raw3)[j]
        mine = packed.at[far, y]
        theirs = ybuf.at[far]
        if j == 0:
            if way == 0:
                pairs = [(mine, pl.ds(0, 2)), (theirs.at[pl.ds(0, 2)], pl.ds(2, 2))]
            else:
                pairs = [(theirs.at[pl.ds(2, 4)], pl.ds(0, 4))]
        else:
            before = (raw1, raw2)[j - 1]
            count = before.shape[1]
            pairs = [(mine, pl.ds(0, 2)), (theirs, pl.ds(2, 6)), (before.at[way], pl.ds(8, count))]
        return [
            remote(a, dst.at[way, b], raw_s.at[way, j, n], raw_r.at[way, j, n], to)
            for n, (a, b) in enumerate(pairs)
        ]

    def cells(g):
        return pl.ds(g * WIDE, WIDE)

    def go(way, j, g):
        return remote(
            dense.at[way, j - 3, cells(g)], dense.at[way, j - 2, cells(g)],
            d_s.at[way, j - 3, g], d_r.at[way, j - 3, g], toward[way],
        )

    def list_cols(far_dest, dz, members):
        there = (z + far_dest) % NZ
        at = (z + dz) % NZ
        return [plan[there // 2 * 2 + child, (y + NY - dy) % NY * NZ + at] for dy, child in members]

    full = [(dy, child) for dy in range(NY) for child in range(2)]

    def own_items(far):
        cols = list_cols(far, 0, full)
        refs = [packed.at[far, y, c] if dy == 0 else ybuf.at[far, 2 * dy - 2 + c] for dy, c in full]
        return list(zip(cols, refs))

    def raw_items(way, far):
        step = NZ - 1 if way == 0 else 1
        last = full[:half_list] if way == 0 else full[half_list:]
        cols = list_cols(far, step, full) + list_cols(far, 2 * step, full) + list_cols(far, 3 * step, last)
        return [(col, raw3.at[way, n]) for n, col in enumerate(cols)]

    def add(total, items, cell):
        for col, ref in items:
            total = total + (col == cell).astype(jnp.float32) * ref[...]
        return total

    def merge(buf, fresh, items, g):
        def one(n, carry):
            cell = g * WIDE + n
            start = jnp.zeros(buf.shape[1:], jnp.float32) if fresh else buf[cell]
            buf[cell] = add(start, items, cell)
            return carry

        lax.fori_loop(0, WIDE, one, 0)

    def strip(body):
        def one(n, carry):
            body(pl.ds(pl.multiple_of(n * SUB, SUB), SUB), n * SUB)
            return carry

        lax.fori_loop(0, lead // SUB, one, 0)

    def places(start, shape):
        row = lax.broadcasted_iota(jnp.int32, shape, 0) + start
        col = lax.broadcasted_iota(jnp.int32, shape, 1)
        return row, col

    def load_lead():
        for zz in range(8):
            x_pass_up(zz).wait_recv()
            x_pass_down(zz).wait_recv()

        def rows_of(at, start):
            block = xbuf[pl.ds(start // rows, SUB // rows)].reshape(SUB, lead)
            lead_ref[at, :] = block
            a_hi[at, :], a_lo[at, :] = split(block)

        strip(rows_of)

    def keep_m(at, value):
        m_ref[at, :] = value
        m_hi[at, :], m_lo[at, :] = split(value)

    def begin():
        def diagonal(at, start):
            row, col = places(start, (SUB, lead))
            t_ref[at, :] = jnp.where(row == col, lead_ref[at, :], 0.0)

        strip(diagonal)
        across = lax.rsqrt(jnp.sum(t_ref[...], axis=0, keepdims=True))

        def rows_of(at, start):
            row, col = places(start, (SUB, lead))
            down = lax.rsqrt(jnp.sum(t_ref[at, :], axis=1, keepdims=True))
            lower = jnp.where(row > col, lead_ref[at, :] * down, 0.0)
            unit = (row == col).astype(jnp.float32)
            diag = jnp.where(row == col, lead_ref[at, :], 0.0) * down * across
            keep_m(at, (unit - lower * across - 0.5 * (diag - unit)) * across)

        strip(rows_of)

    def round_of(exact):
        def pair(high, low):
            return (high, low) if exact else (high,)

        def product(left, right, dims):
            return dot3(left, right, dims) if exact else dot1(left[0], right[0], dims)

        def each(body):
            for n in range(lead // SUB):
                body(pl.ds(n * SUB, SUB), pl.ds(0, (n + 1) * SUB), n * SUB)

        def round_a():
            def rows_of(at, upto, start):
                left = pair(m_hi[at, upto], m_lo[at, upto])
                t_ref[at, upto] = product(left, pair(a_hi[upto, upto], a_lo[upto, upto]), NN)

            each(rows_of)

        def round_b():
            def rows_of(at, upto, start):
                gap = product(split(t_ref[at, upto]), pair(m_hi[upto, upto], m_lo[upto, upto]), NT)
                row, col = places(start, gap.shape)
                g_ref[at, upto] = jnp.where(row > col, gap, jnp.where(row == col, 0.5 * (gap - 1.0), 0.0))

            each(rows_of)

        def round_c():
            def rows_of(at, upto, start):
                fix = product(split(g_ref[at, upto]), pair(m_hi[upto, upto], m_lo[upto, upto]), NN)
                t_ref[at, upto] = m_ref[at, upto] - fix

            each(rows_of)

            def keep(at, upto, start):
                value = t_ref[at, upto]
                m_ref[at, upto] = value
                m_hi[at, upto], m_lo[at, upto] = split(value)

            each(keep)

        return [round_a, round_b, round_c]

    def weigh():
        inverse = (m_hi[...], m_lo[...])
        row, col = places(me * rows, (rows, lead))
        value = dot3(split(xbuf[me]), inverse, NT)
        value = jnp.where(col <= row, value, 0.0)
        out_ref[0, :, :lead] = value
        value = jnp.where(col < row // tile * tile, value, 0.0)
        w_hi[...], w_lo[...] = split(dot3(split(value), inverse, NN))

    def rest_panels():
        for zz in range(8, NZ):
            x_pass_up(zz).wait_recv()
            x_pass_down(zz).wait_recv()

    def subtract(g):
        weights = (w_hi[...], w_lo[...])

        def one(n, carry):
            cell = g * WIDE + n
            block = xbuf[pl.ds(lead // rows + tile // rows * cell, tile // rows)].reshape(tile, lead)
            at = pl.ds(pl.multiple_of(lead + cell * tile, tile), tile)
            out_ref[0, :, at] = -dot3(weights, split(block), NT)
            return carry

        lax.fori_loop(0, WIDE, one, 0)

    todo = [load_lead, begin]
    for n in range(1, ROUNDS):
        todo += round_of(n > COARSE)
    todo += [weigh, rest_panels] + [lambda g=g: subtract(g) for g in range(CHUNKS)]

    def work(count):
        for _ in range(count):
            if todo:
                todo.pop(0)()

    def raw_start(way, j, own):
        copies = raw_go(way, j)
        count = len(copies) if j == 0 else 2
        for copy in copies[:count] if own else copies[count:]:
            copy.start()

    def raw_own(j):
        for way in range(2):
            wait_y(far_of(way, j))
            raw_start(way, j, True)

    def raw_forward(j):
        for way in range(2):
            for copy in raw_go(way, j - 1):
                copy.wait_recv()
        for way in range(2):
            raw_start(way, j, False)

    def packs(*members):
        for far in members:
            pack(far)

    packs(8)
    x_step(2)
    packs(7, 9)
    wait_y(8)
    for way in range(2):
        raw_start(way, 0, True)
    packs(6, 10)
    x_step(3)
    raw_own(1)
    packs(5, 11)
    x_step(4)
    raw_forward(1)
    packs(4, 12)
    x_step(5)
    raw_own(2)
    packs(3, 13)
    x_step(6)
    raw_forward(2)
    packs(2, 14, 1, 15, 0)
    later = []
    for way in range(2):
        far = far_of(way, 3)
        wait_y(far)
        for copy in raw_go(way, 2)[:2]:
            copy.wait_recv()
        lists = raw_items(way, far)
        later.append(lists[8:])
        for g in range(CHUNKS):
            merge(dense.at[way, 0], True, own_items(far) + lists[:8], g)
    x_step(7)
    for way in range(2):
        raw_go(way, 2)[2].wait_recv()
    for g in range(CHUNKS):
        for way in range(2):
            merge(dense.at[way, 0], False, later[way], g)
            go(way, 3, g).start()
        if g == 1:
            x_step(8)
            for zz in range(8):
                x_out(zz)
    outs, passes = list(range(8, NZ)), list(range(NZ))
    for j in range(4, 8):
        for way in range(2):
            wait_y(far_of(way, j))
        items = [own_items(far_of(way, j)) for way in range(2)]
        for g in range(CHUNKS):
            for way in range(2):
                go(way, j - 1, g).wait_recv()
                merge(dense.at[way, j - 3], False, items[way], g)
                go(way, j, g).start()
            slot_at = (j - 4) * CHUNKS + g
            for zz in passes[:2]:
                x_pass(zz)
            del passes[:2]
            for zz in outs[:2]:
                x_out(zz)
            del outs[:2]
            if slot_at > 4:
                work(2 if slot_at < 14 else 3)

    while todo:
        work(1)
    wait_y(0)
    items = own_items(0)
    for g in range(CHUNKS):
        for way in range(2):
            go(way, 7, g).wait_recv()

        def last(n, carry):
            cell = g * WIDE + n
            at = pl.ds(pl.multiple_of(lead + cell * tile, tile), tile)
            total = add(dense[0, 5, cell] + dense[1, 5, cell], items, cell)
            out_ref[0, :, at] = out_ref[0, :, at] + total
            return carry

        lax.fori_loop(0, WIDE, last, 0)

    for zz in range(NZ):
        for copy in (x_up(zz), x_down(zz), x_pass_up(zz), x_pass_down(zz)):
            copy.wait_send()
        for dy in range(1, NY):
            over_y(zz, dy).wait_send()
    for s in range(8):
        x_right(s).wait_send()
        if s < 7:
            x_left(s).wait_send()
    for way in range(2):
        for j in range(3):
            for copy in raw_go(way, j):
                copy.wait_send()
        for j in range(3, 8):
            for g in range(CHUNKS):
                go(way, j, g).wait_send()


def exchange(front, own_tiles, partner_tiles, tile_rows, tile_cols, live, lead):
    rows = front.shape[1]
    tile = own_tiles.shape[-1]
    slots = own_tiles.shape[1]
    sem = pltpu.SemaphoreType.DMA
    any_spec = pl.BlockSpec(memory_space=pl.ANY)
    vmem = pl.BlockSpec(memory_space=pltpu.VMEM)
    f32, bf16 = jnp.float32, jnp.bfloat16
    return pl.pallas_call(
        exchange_kernel,
        out_shape=jax.ShapeDtypeStruct(front.shape, f32),
        in_specs=[any_spec, any_spec, any_spec, vmem, vmem, vmem],
        out_specs=vmem,
        scratch_shapes=[
            pltpu.VMEM((2 * slots + 1, tile, tile), f32),
            pltpu.VMEM((NZ, NY, 2, rows, tile), f32),
            pltpu.VMEM((NZ, 2 * NY - 2, rows, tile), f32),
            pltpu.VMEM((2, 4, rows, tile), f32),
            pltpu.VMEM((2, 12, rows, tile), f32),
            pltpu.VMEM((2, 20, rows, tile), f32),
            pltpu.VMEM((2, 6, CELLS, rows, tile), f32),
            pltpu.VMEM((NY * NZ, rows, lead), f32),
        ]
        + [pltpu.VMEM((24, 128), jnp.int32), pltpu.SMEM((24, 128), jnp.int32)]
        + [pltpu.VMEM((lead, lead), f32)] * 4
        + [pltpu.VMEM((lead, lead), bf16)] * 4
        + [pltpu.VMEM((rows, lead), bf16)] * 2
        + [
            sem((3,)), sem, sem,
            sem((NZ, NY - 1)), sem((NZ, NY - 1)),
            sem((2, 3, 3)), sem((2, 3, 3)),
            sem((2, 5, CHUNKS)), sem((2, 5, CHUNKS)),
            sem((8,)), sem((8,)), sem((7,)), sem((7,)),
        ] + [sem((NZ,))] * 8,
        compiler_params=pltpu.CompilerParams(
            collective_id=0, has_side_effects=True, vmem_limit_bytes=56 * 2**20
        ),
    )(front, own_tiles, partner_tiles, tile_rows, tile_cols, live)


def body(front, own_tiles, partner_tiles, tile_rows, tile_cols, live):
    lead = PANELS * own_tiles.shape[-1]
    tile_rows = tile_rows[:, :, :, 0].transpose(0, 2, 1)
    tile_cols = tile_cols.transpose(0, 2, 1)
    live = live.transpose(0, 2, 1)
    change = exchange(front, own_tiles, partner_tiles, tile_rows, tile_cols, live, lead)
    factored = lax.broadcasted_iota(jnp.int32, change.shape, 2) < lead
    return jnp.where(factored, change, change + front)


def solution(mesh):
    in_specs = (
        P("front", "cube", None),
        P("front", "cube", None, None),
        P("front", "cube", None, None),
        P(),
        P(),
        P(),
    )
    out_specs = P("front", "cube", None)
    return jax.shard_map(body, mesh=mesh, in_specs=in_specs, out_specs=out_specs, check_vma=False)
```
